128 devices in a mesh: row: 16 (over x, y), col: 8 (over z, core).
Axes of the slice: x: 4, y: 4, z: 4, core: 2. Of those that a mesh axis runs over, the one named last changes fastest.
Arguments:
- hidden: bfloat16 [3584, 8192], P('col', 'row'), may hold values from -6 to 6
- down_weight: bfloat16 [8192, 4096], P('row', 'col'), may hold values from -0.0625 to 0.0625
- tokens: bfloat16 [3584, 4096], P(None, 'col'), may hold values from -6 to 6
- layer_scale: bfloat16 [4096], P('col'), may hold values from 0.25 to 1
- merge_weight: bfloat16 [4, 4096, 4096], P(None, 'col', 'row'), may hold values from -0.046875 to 0.046875
- text_embeds: bfloat16 [4096, 4096], P('col', 'row'), may hold values from -6 to 6
- positions: int32 [896], replicated, may hold values from 0 to 4095, as said below
Outputs:
- prompt_states: bfloat16 [4096, 4096], P('col', 'row')
The draws below stay inside these ranges and needn't reach their ends.
Inputs may be any that keep to these rules, and one draw needn't show every extreme that they name: All distinct; the merged rows of each of 28 pictures occupy consecutive positions in their own order, the pictures appear in the prompt in any order, and position 0 holds an image row.
All inputs are finite; a program needn't handle non-finite values.
Results may differ from the reference program's by a relative error of at most 0.0034.
Values may be sent and summed in bfloat16 or wider, within the bound.
A program may use at most 64 MiB of HBM per device.

```python
import jax
import jax.numpy as jnp

D = 4096
FF = 8192
DEC = 4096
PATCHES = 3584
MERGED = 896
PROMPT = 4096
PICS = 28


def draw_positions(key, part):
    text_count = PROMPT - MERGED
    middle = MERGED // 2
    cut_key, order_key, text_key = jax.random.split(jax.random.fold_in(key, 17), 3)
    others = jax.random.permutation(cut_key, MERGED - 2)[:PICS - 2].astype(jnp.int32) + 1
    others = others + (others >= middle).astype(jnp.int32)
    cut_points = jnp.sort(jnp.concatenate([others, jnp.array([middle], dtype=jnp.int32)]))
    firsts = jnp.concatenate([jnp.zeros((1,), jnp.int32), cut_points])
    lasts = jnp.concatenate([cut_points, jnp.array([MERGED], dtype=jnp.int32)])
    pic_sizes = lasts - firsts
    starred = jnp.sum((cut_points <= middle).astype(jnp.int32))
    shuffled = jax.random.permutation(order_key, PICS).astype(jnp.int32)
    slot_index = jnp.arange(PICS, dtype=jnp.int32)
    star_slot = jnp.sum(jnp.where(shuffled == starred, slot_index, 0))
    order = jnp.where(slot_index == 0, starred, jnp.where(slot_index == star_slot, shuffled[0], shuffled))
    gaps = jnp.sort(jax.random.randint(text_key, (PICS,), 0, text_count + 1).astype(jnp.int32))
    gaps = jnp.where(slot_index == 0, 0, gaps)
    ordered_sizes = pic_sizes[order]
    slot_start = jnp.cumsum(ordered_sizes) - ordered_sizes + gaps
    rank = jnp.zeros((PICS,), jnp.int32).at[order].set(slot_index)
    pic_start = slot_start[rank]
    merged_rows = jnp.arange(MERGED, dtype=jnp.int32)
    picture = jnp.sum((merged_rows[:, None] >= cut_points[None, :]).astype(jnp.int32), axis=1)
    return (pic_start[picture] + merged_rows - firsts[picture]).astype(jnp.int32)


def levels(key, dims, pieces, low, largest):
    def one(axis_at, shards_of):
        steps = jax.random.uniform(jax.random.fold_in(jax.random.fold_in(key, 6), axis_at), (shards_of,), jnp.float32, low / len(pieces), largest / len(pieces))
        return jnp.repeat(jnp.exp(steps), dims[axis_at] // shards_of).reshape((-1,) + (1,) * (len(dims) - axis_at - 1))

    gain = one(*pieces[0])
    for cut in pieces[1:]:
        gain = gain * one(*cut)
    return gain


def scatter_about(stream_key, shape, width, most, pieces=(), kind=jnp.bfloat16):
    result = jax.random.normal(stream_key, shape, jnp.float32) * width
    if len(pieces) > 0:
        result = levels(stream_key, shape, pieces, -0.22, 0.18) * result
    return jnp.clip(result, min=-most, max=most).astype(kind)


def setup_inputs(seed: int = 0) -> dict:
    key_list = jax.random.split(jax.random.key(seed), 8)
    return {
        "hidden": scatter_about(key_list[0], (PATCHES, FF), 1.0, 6.0, ((0, 8), (1, 16))),
        "down_weight": scatter_about(key_list[1], (FF, D), FF ** -0.5, 0.0625, ((0, 16), (1, 8))),
        "tokens": scatter_about(key_list[2], (PATCHES, D), 1.0, 6.0, ((1, 8),)),
        "layer_scale": jnp.clip(0.25 + 0.75 * jax.random.uniform(key_list[3], (D,), jnp.float32) ** levels(key_list[3], (D,), ((0, 8),), -0.2, 0.2), 0.25, 1.0).astype(jnp.bfloat16),
        "merge_weight": scatter_about(key_list[4], (4, D, DEC), (4 * D) ** -0.5, 0.046875, ((1, 8), (2, 16))),
        "text_embeds": scatter_about(key_list[5], (PROMPT, DEC), 1.0, 6.0, ((0, 8), (1, 16))),
        "positions": draw_positions(jax.random.fold_in(key_list[7], 71), 0),
    }


def reference(hidden, down_weight, tokens, layer_scale, merge_weight, text_embeds, positions):
    down = jnp.dot(hidden, down_weight, preferred_element_type=jnp.float32)
    vision = (tokens.astype(jnp.float32) + layer_scale.astype(jnp.float32)[None, :] * down).astype(jnp.bfloat16)
    merged = vision.reshape(MERGED, 4 * D)
    projected = jnp.dot(merged, merge_weight.reshape(4 * D, DEC), preferred_element_type=jnp.float32).astype(jnp.bfloat16)
    return text_embeds.at[positions.astype(jnp.int32)].set(projected)
```

```python
import jax
import jax.numpy as jnp
from jax import lax
from jax.experimental import pallas as pl
from jax.experimental.pallas import tpu as pltpu
from jax.sharding import PartitionSpec as P

MESH = pl.DeviceIdType.MESH
BF = jnp.bfloat16
F32 = jnp.float32
CH = 8
ROWS = 448
HALF = 224
TR, TC = 112, 128
MR = 112
CUT = 64
STAGES = 9


def kernel(
    hid, dw, tok_hbm, ls_hbm, mw, txt_hbm, pos_hbm, out,
    H, wd, wm, tok, ls, lsg, txt, pos, perm, choose, keep,
    part, rA1, rA2, sf, sB, rB1, rB2, G, pf, sbuf, R, PB,
    lsem, hs, hr, a1s, a1r, a2s, a2r, b1s, b1r, b2s, b2r,
    c1s, c1r, c2s, c2r, d1s, d1r, d2s, d2r, ps, pr, fs, fr,
):
    row = lax.axis_index("row")
    col = lax.axis_index("col")
    x, y = row // 4, row % 4
    z, k = col // 2, col % 2
    o = 1 - k
    p, q = x + k * (y - x), y + k * (x - y)
    sA, sB_ = 4 - 3 * k, 1 + 3 * k
    zp, zm, zo = (z + 1) % 4, (z + 3) % 4, (z + 2) % 4

    def at_row(r):
        return {"row": r, "col": col}

    def at_col(zz, kk):
        return {"row": row, "col": zz * 2 + kk}

    Ap = at_row(((p + 1) % 4) * sA + q * sB_)
    Am = at_row(((p + 3) % 4) * sA + q * sB_)
    Bp = at_row(p * sA + ((q + 1) % 4) * sB_)
    Bm = at_row(p * sA + ((q + 3) % 4) * sB_)
    partner = at_col(z, o)
    Zp, Zm = at_col(zp, k), at_col(zm, k)
    Zpo, Zmo = at_col(zp, o), at_col(zm, o)
    Z2, Z2o = at_col(zo, k), at_col(zo, o)

    def rcopy(src, dst, ss, rs, dev):
        return pltpu.make_async_remote_copy(
            src_ref=src, dst_ref=dst, send_sem=ss, recv_sem=rs, device_id=dev, device_id_type=MESH
        )

    def block_row(i):
        yh, yl = y // 2, y % 2
        zs = (z + 3 + 2 * yh) % 4
        if i == 0:
            r = (z * 2 + k) * ROWS + y * TR
        elif i == 1:
            r = (z * 2 + o) * ROWS + y * TR
        elif i < 6:
            kk = k if i % 2 == 0 else o
            r = (zs * 2 + kk) * ROWS + (HALF if i >= 4 else 0) + yl * TR
        else:
            r = (zo * 2 + (k if i == 6 else o)) * ROWS + y * TR
        return pl.multiple_of(r, 16)

    lc_h = [
        pltpu.make_async_copy(hid.at[pl.ds(h * HALF, HALF)], H.at[0, pl.ds(h * HALF, HALF)], hr.at[0, h])
        for h in range(2)
    ]
    lc_wd = pltpu.make_async_copy(dw, wd, lsem.at[0])
    lc_wm = pltpu.make_async_copy(mw, wm, lsem.at[1])
    lc_ls = pltpu.make_async_copy(ls_hbm, ls, lsem.at[2])
    lc_txt = pltpu.make_async_copy(txt_hbm, txt, lsem.at[3])
    lc_pos = pltpu.make_async_copy(pos_hbm, pos, lsem.at[4])
    lane0 = pl.multiple_of(x * TC, TC)
    lc_tok = [
        pltpu.make_async_copy(tok_hbm.at[pl.ds(block_row(i), TR), pl.ds(lane0, TC)], tok.at[i], lsem.at[5 + i])
        for i in range(CH)
    ]
    for c in lc_h:
        c.start()
    lc_wd.start()
    lc_pos.start()
    lc_ls.start()
    for c in lc_tok:
        c.start()
    lc_wm.start()
    lc_txt.start()

    barrier = pltpu.get_barrier_semaphore()
    for dev in (partner, Ap, Am, Bp, Bm, Zp, Zm, Zpo, Zmo, Z2, Z2o):
        pl.semaphore_signal(barrier, inc=1, device_id=dev, device_id_type=MESH)
    pl.semaphore_wait(barrier, 11)

    def hpart(h):
        return pl.ds(h * HALF, HALF)

    def send_h(src, i, h, n, dev):
        rcopy(src, H.at[i, hpart(h)], hs.at[n], hr.at[i, h], dev).start()

    send_h(hid.at[hpart(0)], 2, 0, 0, Zp)
    send_h(hid.at[hpart(0)], 2, 1, 1, Zm)
    send_h(hid.at[hpart(0)], 1, 0, 2, partner)
    send_h(hid.at[hpart(1)], 1, 1, 3, partner)
    send_h(hid.at[hpart(1)], 4, 0, 4, Zp)
    send_h(hid.at[hpart(1)], 4, 1, 5, Zm)

    lc_wd.wait()

    ri = lax.broadcasted_iota(jnp.int32, (ROWS, ROWS), 0)
    ci = lax.broadcasted_iota(jnp.int32, (ROWS, ROWS), 1)
    perm[...] = jnp.where((ri % MR) * 4 + ri // MR == ci, 1.0, 0.0).astype(BF)
    lc_ls.wait()
    scale_all = ls[...].astype(F32).reshape(1, 4 * TC)
    for g in range(4):
        lsg[g : g + 1, :] = scale_all[:, g * TC : (g + 1) * TC]

    def slot(a, b):
        hi = b // 2
        g = jnp.where(
            a == 0, 12, jnp.where(a == 1, 8 - 8 * hi, jnp.where(a == 2, 2 * hi, 6 + 2 * hi))
        )
        return g + b

    def rel(xg, yg):
        a = xg + k * (yg - xg)
        b = yg + k * (xg - yg)
        return (a + 4 - p) % 4, (b + 4 - q) % 4

    def stage_m(i):
        for h in range(2):
            rcopy(H.at[i, hpart(h)], H.at[i, hpart(h)], hs.at[0], hr.at[i, h], partner).wait_recv()

        @pl.when(i == 2)
        def _():
            send_h(H.at[2, hpart(0)], 3, 0, 6, partner)
            send_h(H.at[2, hpart(1)], 3, 1, 7, partner)
            send_h(H.at[2, hpart(0)], 6, 0, 8, Zp)

        @pl.when(i == 4)
        def _():
            send_h(H.at[4, hpart(0)], 5, 0, 9, partner)
            send_h(H.at[4, hpart(1)], 5, 1, 10, partner)
            send_h(H.at[4, hpart(1)], 6, 1, 11, Zm)

        @pl.when(i == 6)
        def _():
            send_h(H.at[6, hpart(0)], 7, 0, 12, partner)
            send_h(H.at[6, hpart(1)], 7, 1, 13, partner)

        m = jnp.dot(H[i], wd[...], preferred_element_type=F32)
        for yg in range(4):
            for xg in range(4):
                a, b = rel(xg, yg)
                part[i, slot(a, b)] = m[yg * TR : (yg + 1) * TR, xg * TC : (xg + 1) * TC].astype(BF)
        a1(i)

    def mk_a1(i):
        return (
            rcopy(part.at[i, 0:4], rA1.at[i, 0:4], a1s.at[i, 0], a1r.at[i, 0], Ap),
            rcopy(part.at[i, 4:8], rA1.at[i, 4:8], a1s.at[i, 1], a1r.at[i, 1], Am),
        )

    def mk_a2(i):
        return (
            rcopy(part.at[i, 8:10], rA2.at[i, 0:2], a2s.at[i, 0], a2r.at[i, 0], Ap),
            rcopy(part.at[i, 10:12], rA2.at[i, 2:4], a2s.at[i, 1], a2r.at[i, 1], Am),
        )

    def mk_b1(i):
        return (
            rcopy(sB.at[i, 0], rB1.at[i, 0], b1s.at[i, 0], b1r.at[i, 0], Bp),
            rcopy(sB.at[i, 1], rB1.at[i, 1], b1s.at[i, 1], b1r.at[i, 1], Bm),
        )

    lo, hi_ = pl.ds(0, CUT), pl.ds(CUT, TR - CUT)

    def mk_b2(i):
        return (
            rcopy(sB.at[i, 2, lo], rB2.at[i, lo], b2s.at[i, 0], b2r.at[i, 0], Bp),
            rcopy(sB.at[i, 2, hi_], rB2.at[i, hi_], b2s.at[i, 1], b2r.at[i, 1], Bm),
        )

    def mk_c1(i):
        return (
            rcopy(G.at[i, 0], G.at[i, 3], c1s.at[i, 0], c1r.at[i, 0], Bp),
            rcopy(G.at[i, 0], G.at[i, 1], c1s.at[i, 1], c1r.at[i, 1], Bm),
        )

    def mk_c2(i):
        return (
            rcopy(G.at[i, 3, lo], G.at[i, 2, lo], c2s.at[i, 0], c2r.at[i, 0], Bp),
            rcopy(G.at[i, 1, hi_], G.at[i, 2, hi_], c2s.at[i, 1], c2r.at[i, 1], Bm),
        )

    def mk_d1(i):
        return (
            rcopy(G.at[i, 0:4], G.at[i, 12:16], d1s.at[i, 0], d1r.at[i, 0], Ap),
            rcopy(G.at[i, 0:4], G.at[i, 4:8], d1s.at[i, 1], d1r.at[i, 1], Am),
        )

    def mk_d2(i):
        return (
            rcopy(G.at[i, 12:14], G.at[i, 8:10], d2s.at[i, 0], d2r.at[i, 0], Ap),
            rcopy(G.at[i, 6:8], G.at[i, 10:12], d2s.at[i, 1], d2r.at[i, 1], Am),
        )

    def start(pair):
        for c in pair:
            c.start()

    def arrived(pair):
        for c in pair:
            c.wait_recv()

    def a1(i):
        start(mk_a1(i))

    def stage_a2(i):
        arrived(mk_a1(i))
        for j in range(2):
            part[i, 8 + j] = (part[i, 8 + j].astype(F32) + rA1[i, j].astype(F32)).astype(BF)
            part[i, 10 + j] = (part[i, 10 + j].astype(F32) + rA1[i, 4 + j].astype(F32)).astype(BF)
        start(mk_a2(i))

    def stage_b1(i):
        arrived(mk_a2(i))
        s = []
        for b in range(4):
            direct = rA1[i, 6 + b] if b < 2 else rA1[i, b]
            s.append(part[i, 12 + b].astype(F32) + direct.astype(F32) + rA2[i, b].astype(F32))
        sB[i, 0, :CUT] = s[2][:CUT].astype(BF)
        sB[i, 0, CUT:] = s[1][CUT:].astype(BF)
        sB[i, 1, :CUT] = s[3][:CUT].astype(BF)
        sB[i, 1, CUT:] = s[2][CUT:].astype(BF)
        sf[i, 0] = s[0]
        sf[i, 1, :CUT] = s[1][:CUT]
        sf[i, 1, CUT:] = s[3][CUT:]
        start(mk_b1(i))

    def stage_b2(i):
        arrived(mk_b1(i))
        sB[i, 2, :CUT] = (sf[i, 1, :CUT] + rB1[i, 0, :CUT].astype(F32)).astype(BF)
        sB[i, 2, CUT:] = (sf[i, 1, CUT:] + rB1[i, 1, CUT:].astype(F32)).astype(BF)
        start(mk_b2(i))

    def stage_c1(i):
        arrived(mk_b2(i))
        direct = jnp.concatenate([rB1[i, 1, :CUT].astype(F32), rB1[i, 0, CUT:].astype(F32)], axis=0)
        total = sf[i, 0] + direct + rB2[i].astype(F32)
        pltpu.make_async_copy(tok.at[i], tok.at[i], lsem.at[5 + i]).wait()
        scale = lsg[pl.ds(x, 1), :]
        G[i, 0] = (tok[i].astype(F32) + scale * total).astype(BF)
        start(mk_c1(i))

    def stage_c2(i):
        arrived(mk_c1(i))
        start(mk_c2(i))

    def stage_d1(i):
        arrived(mk_c2(i))
        start(mk_d1(i))

    def stage_d2(i):
        arrived(mk_d1(i))
        start(mk_d2(i))

    def send_p(n, dev):
        rcopy(sbuf.at[n], R.at[n], ps.at[n], pr.at[n], dev).start()

    def stage_e(i):
        arrived(mk_d2(i))
        cols = []
        for xg in range(4):
            tiles = []
            for yg in range(4):
                a, b = rel(xg, yg)
                tiles.append(G[i, a * 4 + b])
            cols.append(jnp.concatenate(tiles, axis=0))
        vision = jnp.concatenate(cols, axis=1)
        sorted_rows = jnp.dot(perm[...], vision, preferred_element_type=F32).astype(BF)

        @pl.when(i == 0)
        def _():
            lc_wm.wait()

        acc = jnp.dot(sorted_rows[:MR], wm[0], preferred_element_type=F32)
        for j in range(1, 4):
            acc = acc + jnp.dot(
                sorted_rows[j * MR : (j + 1) * MR], wm[j], preferred_element_type=F32
            )
        hm = MR // 2

        @pl.when(i == 0)
        def _():
            sbuf[0] = acc.astype(BF)
            send_p(0, Z2o)

        @pl.when(i == 1)
        def _():
            sbuf[1] = acc.astype(BF)
            send_p(1, Z2)

        for first, n, devs in ((2, 2, (Zpo, Zmo)), (3, 4, (Zp, Zm))):

            @pl.when(i == first)
            def _():
                pf[n - 2, :hm] = acc[:hm]
                pf[n - 1, :hm] = acc[hm:]

            @pl.when(i == first + 2)
            def _():
                pf[n - 2, hm:] = acc[:hm]
                pf[n - 1, hm:] = acc[hm:]
                sbuf[n] = pf[n - 2].astype(BF)
                sbuf[n + 1] = pf[n - 1].astype(BF)
                send_p(n, devs[0])
                send_p(n + 1, devs[1])

        @pl.when(i == 6)
        def _():
            sbuf[6] = acc.astype(BF)
            send_p(6, partner)

        @pl.when(i == 7)
        def _():
            pf[4] = acc

    stages = (stage_m, stage_a2, stage_b1, stage_b2, stage_c1, stage_c2, stage_d1, stage_d2, stage_e)
    order = (7, 6, 5, 4, 3, 2, 1, 0, 8)

    def slot_step(t, carry):
        for s in order:
            i = t - s

            @pl.when((i >= 0) & (i < CH))
            def _():
                stages[s](i)

        @pl.when(t == 0)
        def _():
            lc_pos.wait()
            prompt_n = choose.shape[0]
            ids = lax.broadcasted_iota(jnp.int32, choose.shape, 0) + col * prompt_n
            hit = jnp.where(pos[...].reshape(1, choose.shape[1]) == ids, 1.0, 0.0)
            choose[...] = hit.astype(BF)
            keep[...] = jnp.broadcast_to(jnp.max(hit, axis=1, keepdims=True), keep.shape)

        return carry

    lax.fori_loop(0, CH + STAGES - 1, slot_step, 0)

    total = pf[4]
    for n in range(7):
        rcopy(sbuf.at[n], R.at[n], ps.at[n], pr.at[n], partner).wait_recv()
        total = total + R[n].astype(F32)
    own = zo * 2 + o
    PB[own] = total.astype(BF)

    def send_f(src, rows, n, dev):
        c = rcopy(PB.at[src, rows], PB.at[src, rows], fs.at[n], fr.at[n], dev)
        return c

    every = pl.ds(0, MR)
    f_lo, f_hi = pl.ds(0, CUT), pl.ds(CUT, MR - CUT)
    f0 = send_f(own, every, 0, Zp)
    f1 = send_f(own, every, 1, Zm)
    f2 = send_f(own, every, 2, partner)
    for c in (f0, f1, f2):
        c.start()
    from_m, from_p, from_2 = zp * 2 + o, zm * 2 + o, z * 2 + o
    send_f(from_m, every, 0, Zp).wait_recv()
    f3 = send_f(from_m, f_lo, 3, Zp)
    f4 = send_f(from_m, every, 4, partner)
    f3.start()
    f4.start()
    send_f(from_p, every, 1, Zm).wait_recv()
    f5 = send_f(from_p, f_hi, 5, Zm)
    f6 = send_f(from_p, every, 6, partner)
    f5.start()
    f6.start()
    send_f(from_2, f_lo, 3, Zp).wait_recv()
    f7 = send_f(from_2, f_lo, 7, partner)
    f7.start()
    send_f(from_2, f_hi, 5, Zm).wait_recv()
    f8 = send_f(from_2, f_hi, 8, partner)
    f8.start()
    send_f(zo * 2 + k, every, 2, partner).wait_recv()
    send_f(zp * 2 + k, every, 4, partner).wait_recv()
    send_f(zm * 2 + k, every, 6, partner).wait_recv()
    send_f(z * 2 + k, f_lo, 7, partner).wait_recv()
    send_f(z * 2 + k, f_hi, 8, partner).wait_recv()

    lc_txt.wait()
    projected = PB[...].reshape(choose.shape[1], PB.shape[2])
    image = jnp.dot(choose[...], projected, preferred_element_type=F32)
    mask = keep[...]
    for g in range(PB.shape[2] // TC):
        cs = slice(g * TC, (g + 1) * TC)
        out[:, cs] = jnp.where(mask > 0.5, image[:, cs].astype(BF), txt[:, cs])

    for c in (f0, f1, f2, f3, f4, f5, f6, f7, f8):
        c.wait_send()
    for n in range(7):
        rcopy(sbuf.at[n], R.at[n], ps.at[n], pr.at[n], partner).wait_send()
    for n in range(14):
        rcopy(H.at[0, hpart(0)], H.at[0, hpart(0)], hs.at[n], hr.at[0, 0], partner).wait_send()

    def drain(i, carry):
        for mk in (mk_a1, mk_a2, mk_b1, mk_b2, mk_c1, mk_c2, mk_d1, mk_d2):
            for c in mk(i):
                c.wait_send()
        return carry

    lax.fori_loop(0, CH, drain, 0)


def per_device(hidden, down_weight, tokens, layer_scale, merge_weight, text_embeds, positions):
    prompt_n, width = text_embeds.shape
    merged = positions.shape[0]
    dma = pltpu.SemaphoreType.DMA
    vm = pltpu.VMEM
    pair = dma((CH, 2))
    return pl.pallas_call(
        kernel,
        out_shape=jax.ShapeDtypeStruct((prompt_n, width), BF),
        in_specs=[pl.BlockSpec(memory_space=pl.ANY)] * 7,
        out_specs=pl.BlockSpec(memory_space=pltpu.VMEM),
        scratch_shapes=[
            vm((CH, ROWS, hidden.shape[1]), BF),
            vm(down_weight.shape, BF),
            vm(merge_weight.shape, BF),
            vm((CH, TR, TC), BF),
            vm(layer_scale.shape, BF),
            vm((8, TC), F32),
            vm((prompt_n, width), BF),
            vm((merged,), jnp.int32),
            vm((ROWS, ROWS), BF),
            vm((prompt_n, merged), BF),
            vm((prompt_n, TC), F32),
            vm((CH, 16, TR, TC), BF),
            vm((CH, 8, TR, TC), BF),
            vm((CH, 4, TR, TC), BF),
            vm((CH, 2, TR, TC), F32),
            vm((CH, 3, TR, TC), BF),
            vm((CH, 2, TR, TC), BF),
            vm((CH, TR, TC), BF),
            vm((CH, 16, TR, TC), BF),
            vm((5, MR, width), F32),
            vm((7, MR, width), BF),
            vm((7, MR, width), BF),
            vm((8, MR, width), BF),
            dma((13,)),
            dma((14,)),
            pair,
        ]
        + [pair] * 16
        + [dma((7,)), dma((7,)), dma((9,)), dma((9,))],
        compiler_params=pltpu.CompilerParams(
            collective_id=0, has_side_effects=True, vmem_limit_bytes=60 * 1024 * 1024
        ),
    )(hidden, down_weight, tokens, layer_scale, merge_weight, text_embeds, positions)


def solution(mesh):
    in_specs = (
        P("col", "row"),
        P("row", "col"),
        P(None, "col"),
        P("col"),
        P(None, "col", "row"),
        P("col", "row"),
        P(),
    )
    return jax.shard_map(
        per_device, mesh=mesh, in_specs=in_specs, out_specs=P("col", "row"), check_vma=False
    )
```

```python
import jax
import jax.numpy as jnp
from jax import lax
from jax.experimental import pallas as pl
from jax.experimental.pallas import tpu as pltpu
from jax.sharding import PartitionSpec as P

MESH = pl.DeviceIdType.MESH
BF = jnp.bfloat16
F32 = jnp.float32
CH = 8
ROWS = 448
HALF = 224
TR, TC = 112, 128
MR = 112
CUT = 64

ORDER = (
    (0, 0), (1, 0), (0, 1), (1, 1), (2, 0), (0, 2), (3, 0), (1, 2), (0, 3),
    (2, 1), (1, 3), (4, 0), (3, 1), (5, 0), (2, 2), (0, 4), (1, 4), (4, 1),
    (2, 3), (3, 2), (6, 0), (7, 0), (5, 1), (2, 4), (3, 3), (0, 5), (1, 5),
    (4, 2), (6, 1), (2, 5), (3, 4), (0, 6), (1, 6), (7, 1), (4, 3), (2, 6),
    (5, 2), (3, 5), (6, 2), (4, 4), (0, 7), (5, 3), (3, 6), (6, 3), (4, 5),
    (5, 4), (1, 7), (7, 2), (6, 4), (4, 6), (5, 5), (2, 7), (7, 3), (0, 8),
    (6, 5), (5, 6), (7, 4), (3, 7), (1, 8), (6, 6), (4, 7), (7, 5), (2, 8),
    (5, 7), (7, 6), (3, 8), (6, 7), (4, 8), (5, 8), (7, 7), (6, 8), (7, 8),
)


def kernel(
    hid, dw, tok_hbm, ls_hbm, mw, txt_hbm, pos_hbm, out,
    H, wd, wm, tok, ls, lsg, txt, pos, perm, choose, keep,
    part, rA1, rA2, sf, sB, rB1, rB2, G, pf, sbuf, R, PB,
    lsem, hs, hr, a1s, a1r, a2s, a2r, b1s, b1r, b2s, b2r,
    c1s, c1r, c2s, c2r, d1s, d1r, d2s, d2r, ps, pr, fs, fr,
):
    row = lax.axis_index("row")
    col = lax.axis_index("col")
    x, y = row // 4, row % 4
    z, k = col // 2, col % 2
    o = 1 - k
    p, q = x + k * (y - x), y + k * (x - y)
    sA, sB_ = 4 - 3 * k, 1 + 3 * k
    zp, zm, zo = (z + 1) % 4, (z + 3) % 4, (z + 2) % 4

    def at_row(r):
        return {"row": r, "col": col}

    def at_col(zz, kk):
        return {"row": row, "col": zz * 2 + kk}

    Ap = at_row(((p + 1) % 4) * sA + q * sB_)
    Am = at_row(((p + 3) % 4) * sA + q * sB_)
    Bp = at_row(p * sA + ((q + 1) % 4) * sB_)
    Bm = at_row(p * sA + ((q + 3) % 4) * sB_)
    partner = at_col(z, o)
    Zp, Zm = at_col(zp, k), at_col(zm, k)
    Zpo, Zmo = at_col(zp, o), at_col(zm, o)
    Z2, Z2o = at_col(zo, k), at_col(zo, o)

    def rcopy(src, dst, ss, rs, dev):
        return pltpu.make_async_remote_copy(
            src_ref=src, dst_ref=dst, send_sem=ss, recv_sem=rs, device_id=dev, device_id_type=MESH
        )

    def block_row(i):
        yh, yl = y // 2, y % 2
        zs = (z + 3 + 2 * yh) % 4
        if i == 0:
            r = (z * 2 + k) * ROWS + y * TR
        elif i == 1:
            r = (z * 2 + o) * ROWS + y * TR
        elif i < 6:
            kk = k if i % 2 == 0 else o
            r = (zs * 2 + kk) * ROWS + (HALF if i >= 4 else 0) + yl * TR
        else:
            r = (zo * 2 + (k if i == 6 else o)) * ROWS + y * TR
        return pl.multiple_of(r, 16)

    lc_h = [
        pltpu.make_async_copy(hid.at[pl.ds(h * HALF, HALF)], H.at[0, pl.ds(h * HALF, HALF)], hr.at[0, h])
        for h in range(2)
    ]
    lc_wd = pltpu.make_async_copy(dw, wd, lsem.at[0])
    lc_wm = pltpu.make_async_copy(mw, wm, lsem.at[1])
    lc_ls = pltpu.make_async_copy(ls_hbm, ls, lsem.at[2])
    lc_txt = pltpu.make_async_copy(txt_hbm, txt, lsem.at[3])
    lc_pos = pltpu.make_async_copy(pos_hbm, pos, lsem.at[4])
    lane0 = pl.multiple_of(x * TC, TC)
    lc_tok = [
        pltpu.make_async_copy(tok_hbm.at[pl.ds(block_row(i), TR), pl.ds(lane0, TC)], tok.at[i], lsem.at[5 + i])
        for i in range(CH)
    ]
    for c in lc_h:
        c.start()
    lc_wd.start()
    lc_pos.start()
    lc_ls.start()
    for c in lc_tok:
        c.start()
    lc_wm.start()
    lc_txt.start()

    barrier = pltpu.get_barrier_semaphore()
    for dev in (partner, Ap, Am, Bp, Bm, Zp, Zm, Zpo, Zmo, Z2, Z2o):
        pl.semaphore_signal(barrier, inc=1, device_id=dev, device_id_type=MESH)

    def hpart(h):
        return pl.ds(h * HALF, HALF)

    def send_h(src, i, h, n, dev):
        rcopy(src, H.at[i, hpart(h)], hs.at[n], hr.at[i, h], dev).start()

    def slot(a, b):
        hi = b // 2
        g = jnp.where(
            a == 0, 12, jnp.where(a == 1, 8 - 8 * hi, jnp.where(a == 2, 2 * hi, 6 + 2 * hi))
        )
        return g + b

    def rel(xg, yg):
        a = xg + k * (yg - xg)
        b = yg + k * (xg - yg)
        return (a + 4 - p) % 4, (b + 4 - q) % 4

    def multiply(i):
        for h in range(2):
            rcopy(H.at[i, hpart(h)], H.at[i, hpart(h)], hs.at[0], hr.at[i, h], partner).wait_recv()
            if i in (2, 4, 6):
                send_h(H.at[i, hpart(h)], i + 1, h, 5 + i // 2 * 2 - 1 + h, partner)
            if (i, h) == (2, 0):
                send_h(H.at[2, hpart(0)], 6, 0, 12, Zp)
            if (i, h) == (4, 1):
                send_h(H.at[4, hpart(1)], 6, 1, 13, Zm)
        m = jnp.dot(H[i], wd[...], preferred_element_type=F32)
        for yg in range(4):
            for xg in range(4):
                a, b = rel(xg, yg)
                part[i, slot(a, b)] = m[yg * TR : (yg + 1) * TR, xg * TC : (xg + 1) * TC].astype(BF)

    def stage_m(i):
        multiply(i)
        a1(i)

    lc_wd.wait()
    multiply(0)
    pl.semaphore_wait(barrier, 11)
    send_h(hid.at[hpart(0)], 2, 0, 0, Zp)
    send_h(hid.at[hpart(0)], 2, 1, 1, Zm)
    send_h(hid.at[hpart(0)], 1, 0, 2, partner)
    send_h(hid.at[hpart(1)], 1, 1, 3, partner)
    send_h(hid.at[hpart(1)], 4, 0, 4, Zp)
    send_h(hid.at[hpart(1)], 4, 1, 5, Zm)

    def mk_a1(i):
        return (
            rcopy(part.at[i, 0:4], rA1.at[i, 0:4], a1s.at[i, 0], a1r.at[i, 0], Ap),
            rcopy(part.at[i, 4:8], rA1.at[i, 4:8], a1s.at[i, 1], a1r.at[i, 1], Am),
        )

    def mk_a2(i):
        return (
            rcopy(part.at[i, 8:10], rA2.at[i, 0:2], a2s.at[i, 0], a2r.at[i, 0], Ap),
            rcopy(part.at[i, 10:12], rA2.at[i, 2:4], a2s.at[i, 1], a2r.at[i, 1], Am),
        )

    def mk_b1(i):
        return (
            rcopy(sB.at[i, 0], rB1.at[i, 0], b1s.at[i, 0], b1r.at[i, 0], Bp),
            rcopy(sB.at[i, 1], rB1.at[i, 1], b1s.at[i, 1], b1r.at[i, 1], Bm),
        )

    lo, hi_ = pl.ds(0, CUT), pl.ds(CUT, TR - CUT)

    def mk_b2(i):
        return (
            rcopy(sB.at[i, 2, lo], rB2.at[i, lo], b2s.at[i, 0], b2r.at[i, 0], Bp),
            rcopy(sB.at[i, 2, hi_], rB2.at[i, hi_], b2s.at[i, 1], b2r.at[i, 1], Bm),
        )

    def mk_c1(i):
        return (
            rcopy(G.at[i, 0], G.at[i, 3], c1s.at[i, 0], c1r.at[i, 0], Bp),
            rcopy(G.at[i, 0], G.at[i, 1], c1s.at[i, 1], c1r.at[i, 1], Bm),
        )

    def mk_c2(i):
        return (
            rcopy(G.at[i, 3, lo], G.at[i, 2, lo], c2s.at[i, 0], c2r.at[i, 0], Bp),
            rcopy(G.at[i, 1, hi_], G.at[i, 2, hi_], c2s.at[i, 1], c2r.at[i, 1], Bm),
        )

    def mk_d1(i):
        return (
            rcopy(G.at[i, 0:4], G.at[i, 12:16], d1s.at[i, 0], d1r.at[i, 0], Ap),
            rcopy(G.at[i, 0:4], G.at[i, 4:8], d1s.at[i, 1], d1r.at[i, 1], Am),
        )

    def mk_d2(i):
        return (
            rcopy(G.at[i, 12:14], G.at[i, 8:10], d2s.at[i, 0], d2r.at[i, 0], Ap),
            rcopy(G.at[i, 6:8], G.at[i, 10:12], d2s.at[i, 1], d2r.at[i, 1], Am),
        )

    def start(pair):
        for c in pair:
            c.start()

    def arrived(pair):
        for c in pair:
            c.wait_recv()

    def a1(i):
        start(mk_a1(i))

    def stage_a2(i):
        arrived(mk_a1(i))
        for j in range(2):
            part[i, 8 + j] = (part[i, 8 + j].astype(F32) + rA1[i, j].astype(F32)).astype(BF)
            part[i, 10 + j] = (part[i, 10 + j].astype(F32) + rA1[i, 4 + j].astype(F32)).astype(BF)
        start(mk_a2(i))

    def stage_b1(i):
        arrived(mk_a2(i))
        s = []
        for b in range(4):
            direct = rA1[i, 6 + b] if b < 2 else rA1[i, b]
            s.append(part[i, 12 + b].astype(F32) + direct.astype(F32) + rA2[i, b].astype(F32))
        sB[i, 0, :CUT] = s[2][:CUT].astype(BF)
        sB[i, 0, CUT:] = s[1][CUT:].astype(BF)
        sB[i, 1, :CUT] = s[3][:CUT].astype(BF)
        sB[i, 1, CUT:] = s[2][CUT:].astype(BF)
        sf[i, 0] = s[0]
        sf[i, 1, :CUT] = s[1][:CUT]
        sf[i, 1, CUT:] = s[3][CUT:]
        start(mk_b1(i))

    def stage_b2(i):
        arrived(mk_b1(i))
        sB[i, 2, :CUT] = (sf[i, 1, :CUT] + rB1[i, 0, :CUT].astype(F32)).astype(BF)
        sB[i, 2, CUT:] = (sf[i, 1, CUT:] + rB1[i, 1, CUT:].astype(F32)).astype(BF)
        start(mk_b2(i))

    def stage_c1(i):
        arrived(mk_b2(i))
        direct = jnp.concatenate([rB1[i, 1, :CUT].astype(F32), rB1[i, 0, CUT:].astype(F32)], axis=0)
        total = sf[i, 0] + direct + rB2[i].astype(F32)
        pltpu.make_async_copy(tok.at[i], tok.at[i], lsem.at[5 + i]).wait()
        scale = lsg[pl.ds(x, 1), :]
        G[i, 0] = (tok[i].astype(F32) + scale * total).astype(BF)
        start(mk_c1(i))

    def stage_c2(i):
        arrived(mk_c1(i))
        start(mk_c2(i))

    def stage_d1(i):
        arrived(mk_c2(i))
        start(mk_d1(i))

    def stage_d2(i):
        arrived(mk_d1(i))
        start(mk_d2(i))

    def send_p(n, dev):
        rcopy(sbuf.at[n], R.at[n], ps.at[n], pr.at[n], dev).start()

    def stage_e(i):
        arrived(mk_d2(i))
        cols = []
        for xg in range(4):
            tiles = []
            for yg in range(4):
                a, b = rel(xg, yg)
                tiles.append(G[i, a * 4 + b])
            cols.append(jnp.concatenate(tiles, axis=0))
        vision = jnp.concatenate(cols, axis=1)
        sorted_rows = jnp.dot(perm[...], vision, preferred_element_type=F32).astype(BF)

        if not waited:
            waited.append(i)
            lc_wm.wait()

        acc = jnp.dot(sorted_rows[:MR], wm[0], preferred_element_type=F32)
        for j in range(1, 4):
            acc = acc + jnp.dot(
                sorted_rows[j * MR : (j + 1) * MR], wm[j], preferred_element_type=F32
            )
        hm = MR // 2

        if i == 0:
            sbuf[0] = acc.astype(BF)
            send_p(0, Z2o)

        if i == 1:
            sbuf[1] = acc.astype(BF)
            send_p(1, Z2)

        for first, n, devs in ((2, 2, (Zpo, Zmo)), (3, 4, (Zp, Zm))):

            if i == first:
                pf[n - 2, :hm] = acc[:hm]
                pf[n - 1, :hm] = acc[hm:]

            if i == first + 2:
                pf[n - 2, hm:] = acc[:hm]
                pf[n - 1, hm:] = acc[hm:]
                sbuf[n] = pf[n - 2].astype(BF)
                sbuf[n + 1] = pf[n - 1].astype(BF)
                send_p(n, devs[0])
                send_p(n + 1, devs[1])

        if i == 6:
            sbuf[6] = acc.astype(BF)
            send_p(6, partner)

        if i == 7:
            pf[4] = acc

    stages = (stage_m, stage_a2, stage_b1, stage_b2, stage_c1, stage_c2, stage_d1, stage_d2, stage_e)
    waited = []
    a1(0)
    ri = lax.broadcasted_iota(jnp.int32, (ROWS, ROWS), 0)
    ci = lax.broadcasted_iota(jnp.int32, (ROWS, ROWS), 1)
    perm[...] = jnp.where((ri % MR) * 4 + ri // MR == ci, 1.0, 0.0).astype(BF)
    lc_ls.wait()
    scale_all = ls[...].astype(F32).reshape(1, 4 * TC)
    for g in range(4):
        lsg[g : g + 1, :] = scale_all[:, g * TC : (g + 1) * TC]

    lc_pos.wait()
    prompt_n = choose.shape[0]
    ids = lax.broadcasted_iota(jnp.int32, choose.shape, 0) + col * prompt_n
    hit = jnp.where(pos[...].reshape(1, choose.shape[1]) == ids, 1.0, 0.0)
    choose[...] = hit.astype(BF)
    keep[...] = jnp.broadcast_to(jnp.max(hit, axis=1, keepdims=True), keep.shape)

    for i, n in ORDER[1:]:
        stages[n](i)

    total = pf[4]
    for n in range(7):
        rcopy(sbuf.at[n], R.at[n], ps.at[n], pr.at[n], partner).wait_recv()
        total = total + R[n].astype(F32)
    own = zo * 2 + o
    PB[own] = total.astype(BF)

    def send_f(src, rows, n, dev):
        c = rcopy(PB.at[src, rows], PB.at[src, rows], fs.at[n], fr.at[n], dev)
        return c

    every = pl.ds(0, MR)
    f_lo, f_hi = pl.ds(0, CUT), pl.ds(CUT, MR - CUT)
    f0 = send_f(own, every, 0, Zp)
    f1 = send_f(own, every, 1, Zm)
    f2 = send_f(own, every, 2, partner)
    for c in (f0, f1, f2):
        c.start()
    from_m, from_p, from_2 = zp * 2 + o, zm * 2 + o, z * 2 + o
    send_f(from_m, every, 0, Zp).wait_recv()
    f3 = send_f(from_m, f_lo, 3, Zp)
    f4 = send_f(from_m, every, 4, partner)
    f3.start()
    f4.start()
    send_f(from_p, every, 1, Zm).wait_recv()
    f5 = send_f(from_p, f_hi, 5, Zm)
    f6 = send_f(from_p, every, 6, partner)
    f5.start()
    f6.start()
    send_f(from_2, f_lo, 3, Zp).wait_recv()
    f7 = send_f(from_2, f_lo, 7, partner)
    f7.start()
    send_f(from_2, f_hi, 5, Zm).wait_recv()
    f8 = send_f(from_2, f_hi, 8, partner)
    f8.start()
    send_f(zo * 2 + k, every, 2, partner).wait_recv()
    send_f(zp * 2 + k, every, 4, partner).wait_recv()
    send_f(zm * 2 + k, every, 6, partner).wait_recv()
    send_f(z * 2 + k, f_lo, 7, partner).wait_recv()
    send_f(z * 2 + k, f_hi, 8, partner).wait_recv()

    lc_txt.wait()
    projected = PB[...].reshape(choose.shape[1], PB.shape[2])
    image = jnp.dot(choose[...], projected, preferred_element_type=F32)
    mask = keep[...]
    for g in range(PB.shape[2] // TC):
        cs = slice(g * TC, (g + 1) * TC)
        out[:, cs] = jnp.where(mask > 0.5, image[:, cs].astype(BF), txt[:, cs])

    for c in (f0, f1, f2, f3, f4, f5, f6, f7, f8):
        c.wait_send()
    for n in range(7):
        rcopy(sbuf.at[n], R.at[n], ps.at[n], pr.at[n], partner).wait_send()
    for n in range(14):
        rcopy(H.at[0, hpart(0)], H.at[0, hpart(0)], hs.at[n], hr.at[0, 0], partner).wait_send()

    def drain(i, carry):
        for mk in (mk_a1, mk_a2, mk_b1, mk_b2, mk_c1, mk_c2, mk_d1, mk_d2):
            for c in mk(i):
                c.wait_send()
        return carry

    lax.fori_loop(0, CH, drain, 0)


def per_device(hidden, down_weight, tokens, layer_scale, merge_weight, text_embeds, positions):
    prompt_n, width = text_embeds.shape
    merged = positions.shape[0]
    dma = pltpu.SemaphoreType.DMA
    vm = pltpu.VMEM
    pair = dma((CH, 2))
    return pl.pallas_call(
        kernel,
        out_shape=jax.ShapeDtypeStruct((prompt_n, width), BF),
        in_specs=[pl.BlockSpec(memory_space=pl.ANY)] * 7,
        out_specs=pl.BlockSpec(memory_space=pltpu.VMEM),
        scratch_shapes=[
            vm((CH, ROWS, hidden.shape[1]), BF),
            vm(down_weight.shape, BF),
            vm(merge_weight.shape, BF),
            vm((CH, TR, TC), BF),
            vm(layer_scale.shape, BF),
            vm((8, TC), F32),
            vm((prompt_n, width), BF),
            vm((merged,), jnp.int32),
            vm((ROWS, ROWS), BF),
            vm((prompt_n, merged), BF),
            vm((prompt_n, TC), F32),
            vm((CH, 16, TR, TC), BF),
            vm((CH, 8, TR, TC), BF),
            vm((CH, 4, TR, TC), BF),
            vm((CH, 2, TR, TC), F32),
            vm((CH, 3, TR, TC), BF),
            vm((CH, 2, TR, TC), BF),
            vm((CH, TR, TC), BF),
            vm((CH, 16, TR, TC), BF),
            vm((5, MR, width), F32),
            vm((7, MR, width), BF),
            vm((7, MR, width), BF),
            vm((8, MR, width), BF),
            dma((13,)),
            dma((14,)),
            pair,
        ]
        + [pair] * 16
        + [dma((7,)), dma((7,)), dma((9,)), dma((9,))],
        compiler_params=pltpu.CompilerParams(
            collective_id=0, has_side_effects=True, vmem_limit_bytes=60 * 1024 * 1024
        ),
    )(hidden, down_weight, tokens, layer_scale, merge_weight, text_embeds, positions)


def solution(mesh):
    in_specs = (
        P("col", "row"),
        P("row", "col"),
        P(None, "col"),
        P("col"),
        P(None, "col", "row"),
        P("col", "row"),
        P(),
    )
    return jax.shard_map(
        per_device, mesh=mesh, in_specs=in_specs, out_specs=P("col", "row"), check_vma=False
    )
```

```python
import jax
import jax.numpy as jnp
from jax import lax
from jax.experimental import pallas as pl
from jax.experimental.pallas import tpu as pltpu
from jax.sharding import PartitionSpec as P

MESH = pl.DeviceIdType.MESH
BF = jnp.bfloat16
F32 = jnp.float32
CH = 8
ROWS = 448
HALF = 224
TR, TC = 112, 128
MR = 112

ORDER = (
    (0, 0), (1, 0), (0, 1), (1, 1), (2, 0), (3, 0), (0, 2), (1, 2), (2, 1),
    (4, 0), (5, 0), (1, 3), (2, 2), (0, 3), (3, 1), (4, 1), (6, 0), (7, 0),
    (5, 1), (3, 2), (0, 4), (6, 1), (1, 4), (4, 2), (2, 3), (7, 1), (3, 3),
    (0, 5), (5, 2), (4, 3), (2, 4), (6, 2), (1, 5), (7, 2), (5, 3), (3, 4),
    (0, 6), (4, 4), (2, 5), (6, 3), (7, 3), (1, 6), (5, 4), (3, 5), (4, 5),
    (6, 4), (2, 6), (7, 4), (5, 5), (3, 6), (6, 5), (4, 6), (7, 5), (5, 6),
    (6, 6), (7, 6),
)


def kernel(
    hid, dw, tok_hbm, ls_hbm, mw, txt_hbm, pos_hbm, out,
    H, wd, wm, tok, ls, lsg, txt, pos, perm, choose, keep,
    part, rA1, rA2, sf, sB, rB, G, pf, sbuf, R, PB,
    lsem, hs, hr, a1s, a1r, a2s, a2r, bs, br,
    cs_, cr, d1s, d1r, d2s, d2r, ps, pr, fs, fr,
):
    row = lax.axis_index("row")
    col = lax.axis_index("col")
    x, y = row // 4, row % 4
    z, k = col // 2, col % 2
    o = 1 - k
    p, q = x + k * (y - x), y + k * (x - y)
    sA, sB_ = 4 - 3 * k, 1 + 3 * k
    zp, zm, zo = (z + 1) % 4, (z + 3) % 4, (z + 2) % 4

    def at_row(r):
        return {"row": r, "col": col}

    def at_col(zz, kk):
        return {"row": row, "col": zz * 2 + kk}

    Ap = at_row(((p + 1) % 4) * sA + q * sB_)
    Am = at_row(((p + 3) % 4) * sA + q * sB_)
    Bp = at_row(p * sA + ((q + 1) % 4) * sB_)
    Bm = at_row(p * sA + ((q + 3) % 4) * sB_)
    B2 = at_row(p * sA + ((q + 2) % 4) * sB_)
    partner = at_col(z, o)
    Zp, Zm = at_col(zp, k), at_col(zm, k)
    Zpo, Zmo = at_col(zp, o), at_col(zm, o)
    Z2, Z2o = at_col(zo, k), at_col(zo, o)

    def rcopy(src, dst, ss, rs, dev):
        return pltpu.make_async_remote_copy(
            src_ref=src, dst_ref=dst, send_sem=ss, recv_sem=rs, device_id=dev, device_id_type=MESH
        )

    def block_row(i):
        yh, yl = y // 2, y % 2
        zs = (z + 3 + 2 * yh) % 4
        if i == 0:
            r = (z * 2 + k) * ROWS + y * TR
        elif i == 1:
            r = (z * 2 + o) * ROWS + y * TR
        elif i < 6:
            kk = k if i % 2 == 0 else o
            r = (zs * 2 + kk) * ROWS + (HALF if i >= 4 else 0) + yl * TR
        else:
            r = (zo * 2 + (k if i == 6 else o)) * ROWS + y * TR
        return pl.multiple_of(r, 16)

    lc_h = [
        pltpu.make_async_copy(hid.at[pl.ds(h * HALF, HALF)], H.at[0, pl.ds(h * HALF, HALF)], hr.at[0, h])
        for h in range(2)
    ]
    lc_wd = pltpu.make_async_copy(dw, wd, lsem.at[0])
    lc_wm = pltpu.make_async_copy(mw, wm, lsem.at[1])
    lc_ls = pltpu.make_async_copy(ls_hbm, ls, lsem.at[2])
    lc_txt = pltpu.make_async_copy(txt_hbm, txt, lsem.at[3])
    lc_pos = pltpu.make_async_copy(pos_hbm, pos, lsem.at[4])
    lane0 = pl.multiple_of(x * TC, TC)
    lc_tok = [
        pltpu.make_async_copy(tok_hbm.at[pl.ds(block_row(i), TR), pl.ds(lane0, TC)], tok.at[i], lsem.at[5 + i])
        for i in range(CH)
    ]
    for c in lc_h:
        c.start()
    lc_wd.start()
    lc_pos.start()
    lc_ls.start()
    for c in lc_tok:
        c.start()
    lc_wm.start()
    lc_txt.start()

    barrier = pltpu.get_barrier_semaphore()
    for dev in (partner, Ap, Am, Bp, Bm, B2, Zp, Zm, Zpo, Zmo, Z2, Z2o):
        pl.semaphore_signal(barrier, inc=1, device_id=dev, device_id_type=MESH)

    def hpart(h):
        return pl.ds(h * HALF, HALF)

    def send_h(src, i, h, n, dev):
        rcopy(src, H.at[i, hpart(h)], hs.at[n], hr.at[i, h], dev).start()

    def slot(a, b):
        hi = b // 2
        g = jnp.where(
            a == 0, 12, jnp.where(a == 1, 8 - 8 * hi, jnp.where(a == 2, 2 * hi, 6 + 2 * hi))
        )
        return g + b

    def rel(xg, yg):
        a = xg + k * (yg - xg)
        b = yg + k * (xg - yg)
        return (a + 4 - p) % 4, (b + 4 - q) % 4

    def multiply(i):
        for h in range(2):
            rcopy(H.at[i, hpart(h)], H.at[i, hpart(h)], hs.at[0], hr.at[i, h], partner).wait_recv()
            if i in (2, 4, 6):
                send_h(H.at[i, hpart(h)], i + 1, h, 5 + i // 2 * 2 - 1 + h, partner)
            if (i, h) == (2, 0):
                send_h(H.at[2, hpart(0)], 6, 0, 12, Zp)
            if (i, h) == (4, 1):
                send_h(H.at[4, hpart(1)], 6, 1, 13, Zm)
        m = jnp.dot(H[i], wd[...], preferred_element_type=F32)
        for yg in range(4):
            for xg in range(4):
                a, b = rel(xg, yg)
                part[i, slot(a, b)] = m[yg * TR : (yg + 1) * TR, xg * TC : (xg + 1) * TC].astype(BF)

    def stage_m(i):
        multiply(i)
        a1(i)

    lc_wd.wait()
    multiply(0)
    pl.semaphore_wait(barrier, 12)
    send_h(hid.at[hpart(0)], 2, 0, 0, Zp)
    send_h(hid.at[hpart(0)], 2, 1, 1, Zm)
    send_h(hid.at[hpart(0)], 1, 0, 2, partner)
    send_h(hid.at[hpart(1)], 1, 1, 3, partner)
    send_h(hid.at[hpart(1)], 4, 0, 4, Zp)
    send_h(hid.at[hpart(1)], 4, 1, 5, Zm)

    def mk_a1(i):
        return (
            rcopy(part.at[i, 0:4], rA1.at[i, 0:4], a1s.at[i, 0], a1r.at[i, 0], Ap),
            rcopy(part.at[i, 4:8], rA1.at[i, 4:8], a1s.at[i, 1], a1r.at[i, 1], Am),
        )

    def mk_a2(i):
        return (
            rcopy(part.at[i, 8:10], rA2.at[i, 0:2], a2s.at[i, 0], a2r.at[i, 0], Ap),
            rcopy(part.at[i, 10:12], rA2.at[i, 2:4], a2s.at[i, 1], a2r.at[i, 1], Am),
        )

    def mk_b(i):
        return tuple(
            rcopy(sB.at[i, j], rB.at[i, j], bs.at[i, j], br.at[i, j], dev)
            for j, dev in enumerate((Bp, Bm, B2))
        )

    def mk_c(i):
        return tuple(
            rcopy(G.at[i, 0], G.at[i, j], cs_.at[i, n], cr.at[i, n], dev)
            for n, (j, dev) in enumerate(((3, Bp), (1, Bm), (2, B2)))
        )

    def mk_d1(i):
        return (
            rcopy(G.at[i, 0:4], G.at[i, 12:16], d1s.at[i, 0], d1r.at[i, 0], Ap),
            rcopy(G.at[i, 0:4], G.at[i, 4:8], d1s.at[i, 1], d1r.at[i, 1], Am),
        )

    def mk_d2(i):
        return (
            rcopy(G.at[i, 12:14], G.at[i, 8:10], d2s.at[i, 0], d2r.at[i, 0], Ap),
            rcopy(G.at[i, 6:8], G.at[i, 10:12], d2s.at[i, 1], d2r.at[i, 1], Am),
        )

    def start(pair):
        for c in pair:
            c.start()

    def arrived(pair):
        for c in pair:
            c.wait_recv()

    def a1(i):
        start(mk_a1(i))

    def stage_a2(i):
        arrived(mk_a1(i))
        for j in range(2):
            part[i, 8 + j] = (part[i, 8 + j].astype(F32) + rA1[i, j].astype(F32)).astype(BF)
            part[i, 10 + j] = (part[i, 10 + j].astype(F32) + rA1[i, 4 + j].astype(F32)).astype(BF)
        start(mk_a2(i))

    def stage_b(i):
        arrived(mk_a2(i))
        for b in range(4):
            direct = rA1[i, 6 + b] if b < 2 else rA1[i, b]
            total = part[i, 12 + b].astype(F32) + direct.astype(F32) + rA2[i, b].astype(F32)
            if b == 0:
                sf[i] = total
            else:
                sB[i, (None, 0, 2, 1)[b]] = total.astype(BF)
        start(mk_b(i))

    def stage_c(i):
        arrived(mk_b(i))
        total = sf[i] + rB[i, 0].astype(F32) + rB[i, 1].astype(F32) + rB[i, 2].astype(F32)
        lc_tok[i].wait()
        scale = lsg[pl.ds(x, 1), :]
        G[i, 0] = (tok[i].astype(F32) + scale * total).astype(BF)
        start(mk_c(i))

    def stage_d1(i):
        arrived(mk_c(i))
        start(mk_d1(i))

    def stage_d2(i):
        arrived(mk_d1(i))
        start(mk_d2(i))

    def send_p(n, dev):
        rcopy(sbuf.at[n], R.at[n], ps.at[n], pr.at[n], dev).start()

    def stage_e(i):
        arrived(mk_d2(i))
        cols = []
        for xg in range(4):
            tiles = []
            for yg in range(4):
                a, b = rel(xg, yg)
                tiles.append(G[i, a * 4 + b])
            cols.append(jnp.concatenate(tiles, axis=0))
        vision = jnp.concatenate(cols, axis=1)
        sorted_rows = jnp.dot(perm[...], vision, preferred_element_type=F32).astype(BF)

        if not waited:
            waited.append(i)
            lc_wm.wait()

        acc = jnp.dot(sorted_rows[:MR], wm[0], preferred_element_type=F32)
        for j in range(1, 4):
            acc = acc + jnp.dot(
                sorted_rows[j * MR : (j + 1) * MR], wm[j], preferred_element_type=F32
            )
        hm = MR // 2

        if i == 0:
            sbuf[0] = acc.astype(BF)
            send_p(0, Z2o)

        if i == 1:
            sbuf[1] = acc.astype(BF)
            send_p(1, Z2)

        for first, n, devs in ((2, 2, (Zpo, Zmo)), (3, 4, (Zp, Zm))):

            if i == first:
                pf[n - 2, :hm] = acc[:hm]
                pf[n - 1, :hm] = acc[hm:]

            if i == first + 2:
                pf[n - 2, hm:] = acc[:hm]
                pf[n - 1, hm:] = acc[hm:]
                sbuf[n] = pf[n - 2].astype(BF)
                sbuf[n + 1] = pf[n - 1].astype(BF)
                send_p(n, devs[0])
                send_p(n + 1, devs[1])

        if i == 6:
            sbuf[6] = acc.astype(BF)
            send_p(6, partner)

        if i == 7:
            pf[4] = acc

    stages = (stage_m, stage_a2, stage_b, stage_c, stage_d1, stage_d2, stage_e)
    waited = []
    a1(0)
    ri = lax.broadcasted_iota(jnp.int32, (ROWS, ROWS), 0)
    ci = lax.broadcasted_iota(jnp.int32, (ROWS, ROWS), 1)
    perm[...] = jnp.where((ri % MR) * 4 + ri // MR == ci, 1.0, 0.0).astype(BF)
    lc_ls.wait()
    scale_all = ls[...].astype(F32).reshape(1, 4 * TC)
    for g in range(4):
        lsg[g : g + 1, :] = scale_all[:, g * TC : (g + 1) * TC]

    lc_pos.wait()
    prompt_n = choose.shape[0]
    ids = lax.broadcasted_iota(jnp.int32, choose.shape, 0) + col * prompt_n
    hit = jnp.where(pos[...].reshape(1, choose.shape[1]) == ids, 1.0, 0.0)
    choose[...] = hit.astype(BF)
    keep[...] = jnp.broadcast_to(jnp.max(hit, axis=1, keepdims=True), keep.shape)

    for i, n in ORDER[1:]:
        stages[n](i)

    total = pf[4]
    for n in range(7):
        rcopy(sbuf.at[n], R.at[n], ps.at[n], pr.at[n], partner).wait_recv()
        total = total + R[n].astype(F32)
    own = zo * 2 + o
    PB[own] = total.astype(BF)

    def send_f(src, rows, n, dev):
        c = rcopy(PB.at[src, rows], PB.at[src, rows], fs.at[n], fr.at[n], dev)
        return c

    every = pl.ds(0, MR)
    sent = [send_f(own, every, n, dev) for n, dev in enumerate((Zp, Zm, Z2, partner))]
    for c in sent:
        c.start()
    for n, dev, block in ((0, Zp, zp), (1, Zm, zm), (2, Z2, z)):
        send_f(block * 2 + o, every, n, dev).wait_recv()
        onward = send_f(block * 2 + o, every, 4 + n, partner)
        onward.start()
        sent.append(onward)
    for n, block in ((3, zo), (4, zp), (5, zm), (6, z)):
        send_f(block * 2 + k, every, n, partner).wait_recv()

    lc_txt.wait()
    projected = PB[...].reshape(choose.shape[1], PB.shape[2])
    image = jnp.dot(choose[...], projected, preferred_element_type=F32)
    mask = keep[...]
    for g in range(PB.shape[2] // TC):
        cs = slice(g * TC, (g + 1) * TC)
        out[:, cs] = jnp.where(mask > 0.5, image[:, cs].astype(BF), txt[:, cs])

    for c in sent:
        c.wait_send()
    for n in range(7):
        rcopy(sbuf.at[n], R.at[n], ps.at[n], pr.at[n], partner).wait_send()
    for n in range(14):
        rcopy(H.at[0, hpart(0)], H.at[0, hpart(0)], hs.at[n], hr.at[0, 0], partner).wait_send()

    def drain(i, carry):
        for mk in (mk_a1, mk_a2, mk_b, mk_c, mk_d1, mk_d2):
            for c in mk(i):
                c.wait_send()
        return carry

    lax.fori_loop(0, CH, drain, 0)


def per_device(hidden, down_weight, tokens, layer_scale, merge_weight, text_embeds, positions):
    prompt_n, width = text_embeds.shape
    merged = positions.shape[0]
    dma = pltpu.SemaphoreType.DMA
    vm = pltpu.VMEM
    pair = dma((CH, 2))
    return pl.pallas_call(
        kernel,
        out_shape=jax.ShapeDtypeStruct((prompt_n, width), BF),
        in_specs=[pl.BlockSpec(memory_space=pl.ANY)] * 7,
        out_specs=pl.BlockSpec(memory_space=pltpu.VMEM),
        scratch_shapes=[
            vm((CH, ROWS, hidden.shape[1]), BF),
            vm(down_weight.shape, BF),
            vm(merge_weight.shape, BF),
            vm((CH, TR, TC), BF),
            vm(layer_scale.shape, BF),
            vm((8, TC), F32),
            vm((prompt_n, width), BF),
            vm((merged,), jnp.int32),
            vm((ROWS, ROWS), BF),
            vm((prompt_n, merged), BF),
            vm((prompt_n, TC), F32),
            vm((CH, 16, TR, TC), BF),
            vm((CH, 8, TR, TC), BF),
            vm((CH, 4, TR, TC), BF),
            vm((CH, TR, TC), F32),
            vm((CH, 3, TR, TC), BF),
            vm((CH, 3, TR, TC), BF),
            vm((CH, 16, TR, TC), BF),
            vm((5, MR, width), F32),
            vm((7, MR, width), BF),
            vm((7, MR, width), BF),
            vm((8, MR, width), BF),
            dma((13,)),
            dma((14,)),
            pair,
        ]
        + [pair] * 4
        + [dma((CH, 3))] * 4
        + [pair] * 4
        + [dma((7,))] * 4,
        compiler_params=pltpu.CompilerParams(
            collective_id=0, has_side_effects=True, vmem_limit_bytes=60 * 1024 * 1024
        ),
    )(hidden, down_weight, tokens, layer_scale, merge_weight, text_embeds, positions)


def solution(mesh):
    in_specs = (
        P("col", "row"),
        P("row", "col"),
        P(None, "col"),
        P("col"),
        P(None, "col", "row"),
        P("col", "row"),
        P(),
    )
    return jax.shard_map(
        per_device, mesh=mesh, in_specs=in_specs, out_specs=P("col", "row"), check_vma=False
    )
```

```python
import jax
import jax.numpy as jnp
from jax import lax
from jax.experimental import pallas as pl
from jax.experimental.pallas import tpu as pltpu
from jax.sharding import PartitionSpec as P

MESH = pl.DeviceIdType.MESH
BF = jnp.bfloat16
F32 = jnp.float32
CH = 8
ROWS = 448
HALF = 224
TR, TC = 112, 128
MR = 112

ORDER = (
    (0, 0), (1, 0), (1, 1), (0, 1), (2, 0), (3, 0), (0, 2), (1, 2), (2, 1),
    (4, 0), (3, 1), (5, 0), (0, 3), (1, 3), (2, 2), (6, 0), (4, 1), (7, 0),
    (0, 4), (5, 1), (1, 4), (3, 2), (2, 3), (6, 1), (7, 1), (4, 2), (0, 5),
    (3, 3), (2, 4), (5, 2), (4, 3), (6, 2), (7, 2), (3, 4), (1, 5), (0, 6),
    (5, 3), (4, 4), (2, 5), (6, 3), (7, 3), (3, 5), (5, 4), (1, 6), (4, 5),
    (6, 4), (2, 6), (7, 4), (3, 6), (5, 5), (4, 6), (6, 5), (7, 5), (5, 6),
    (6, 6), (7, 6),
)


def kernel(
    hid, dw, tok_hbm, ls_hbm, mw, txt_hbm, pos_hbm, out,
    H, wd, wm, tok, ls, lsg, txt, pos, perm, choose, keep,
    part, rA1, rA2, sf, sB, rB, G, pf, sbuf, R, PB,
    lsem, hs, hr, a1s, a1r, a2s, a2r, bs, br,
    cs_, cr, d1s, d1r, d2s, d2r, ps, pr, fs, fr, beyond,
):
    row = lax.axis_index("row")
    col = lax.axis_index("col")
    x, y = row // 4, row % 4
    z, k = col // 2, col % 2
    o = 1 - k
    p, q = x + k * (y - x), y + k * (x - y)
    sA, sB_ = 4 - 3 * k, 1 + 3 * k
    zp, zm, zo = (z + 1) % 4, (z + 3) % 4, (z + 2) % 4

    def at_row(r):
        return {"row": r, "col": col}

    def at_col(zz, kk):
        return {"row": row, "col": zz * 2 + kk}

    Ap = at_row(((p + 1) % 4) * sA + q * sB_)
    Am = at_row(((p + 3) % 4) * sA + q * sB_)
    Bp = at_row(p * sA + ((q + 1) % 4) * sB_)
    Bm = at_row(p * sA + ((q + 3) % 4) * sB_)
    B2 = at_row(p * sA + ((q + 2) % 4) * sB_)
    partner = at_col(z, o)
    Zp, Zm = at_col(zp, k), at_col(zm, k)
    Zpo, Zmo = at_col(zp, o), at_col(zm, o)
    Z2, Z2o = at_col(zo, k), at_col(zo, o)

    def rcopy(src, dst, ss, rs, dev):
        return pltpu.make_async_remote_copy(
            src_ref=src, dst_ref=dst, send_sem=ss, recv_sem=rs, device_id=dev, device_id_type=MESH
        )

    def block_row(i):
        yh, yl = y // 2, y % 2
        zs = (z + 3 + 2 * yh) % 4
        if i == 0:
            r = (z * 2 + k) * ROWS + y * TR
        elif i == 1:
            r = (z * 2 + o) * ROWS + y * TR
        elif i < 6:
            kk = k if i % 2 == 0 else o
            r = (zs * 2 + kk) * ROWS + ((yh + i // 4) % 2) * HALF + yl * TR
        else:
            r = (zo * 2 + (k if i == 6 else o)) * ROWS + y * TR
        return pl.multiple_of(r, 16)

    lc_h = [
        pltpu.make_async_copy(hid.at[pl.ds(h * HALF, HALF)], H.at[0, pl.ds(h * HALF, HALF)], hr.at[0, h])
        for h in range(2)
    ]
    lc_wd = pltpu.make_async_copy(dw, wd, lsem.at[0])
    lc_wm = pltpu.make_async_copy(mw, wm, lsem.at[1])
    lc_ls = pltpu.make_async_copy(ls_hbm, ls, lsem.at[2])
    lc_txt = pltpu.make_async_copy(txt_hbm, txt, lsem.at[3])
    lc_pos = pltpu.make_async_copy(pos_hbm, pos, lsem.at[4])
    lane0 = pl.multiple_of(x * TC, TC)
    lc_tok = [
        pltpu.make_async_copy(tok_hbm.at[pl.ds(block_row(i), TR), pl.ds(lane0, TC)], tok.at[i], lsem.at[5 + i])
        for i in range(CH)
    ]
    for c in lc_h:
        c.start()
    lc_wd.start()
    lc_pos.start()
    lc_ls.start()
    for c in lc_tok:
        c.start()
    lc_wm.start()
    lc_txt.start()

    barrier = pltpu.get_barrier_semaphore()
    for dev in (partner, Ap, Am, Bp, Bm, Zp, Zm):
        pl.semaphore_signal(barrier, inc=1, device_id=dev, device_id_type=MESH)

    def hpart(h):
        return pl.ds(h * HALF, HALF)

    def send_h(src, i, h, n, dev):
        rcopy(src, H.at[i, hpart(h)], hs.at[n], hr.at[i, h], dev).start()

    def slot(a, b):
        hi = b // 2
        g = jnp.where(
            a == 0, 12, jnp.where(a == 1, 8 - 8 * hi, jnp.where(a == 2, 2 * hi, 6 + 2 * hi))
        )
        return g + b

    def rel(xg, yg):
        a = xg + k * (yg - xg)
        b = yg + k * (xg - yg)
        return (a + 4 - p) % 4, (b + 4 - q) % 4

    def multiply(i):
        for h in range(2):
            rcopy(H.at[i, hpart(h)], H.at[i, hpart(h)], hs.at[0], hr.at[i, h], partner).wait_recv()
            if i in (2, 4, 6):
                send_h(H.at[i, hpart(h)], i + 1, h, 5 + i // 2 * 2 - 1 + h, partner)
            if i == 2:
                send_h(H.at[2, hpart(h)], 6, h, 12 + h, (Zp, Zm)[h])
        m = jnp.dot(H[i], wd[...], preferred_element_type=F32)
        for yg in range(4):
            for xg in range(4):
                a, b = rel(xg, yg)
                part[i, slot(a, b)] = m[yg * TR : (yg + 1) * TR, xg * TC : (xg + 1) * TC].astype(BF)

    def stage_m(i):
        multiply(i)
        a1(i)

    lc_wd.wait()
    multiply(0)
    pl.semaphore_wait(barrier, 7)
    send_h(hid.at[hpart(0)], 2, 0, 0, Zp)
    send_h(hid.at[hpart(1)], 2, 1, 1, Zm)
    send_h(hid.at[hpart(0)], 1, 0, 2, partner)
    send_h(hid.at[hpart(1)], 1, 1, 3, partner)
    send_h(hid.at[hpart(1)], 4, 0, 4, Zp)
    send_h(hid.at[hpart(0)], 4, 1, 5, Zm)

    for dev in (Bp, Bm):
        pl.semaphore_signal(beyond, inc=1, device_id=dev, device_id_type=MESH)

    def mk_a1(i):
        return (
            rcopy(part.at[i, 0:4], rA1.at[i, 0:4], a1s.at[i, 0], a1r.at[i, 0], Ap),
            rcopy(part.at[i, 4:8], rA1.at[i, 4:8], a1s.at[i, 1], a1r.at[i, 1], Am),
        )

    def mk_a2(i):
        return (
            rcopy(part.at[i, 8:10], rA2.at[i, 0:2], a2s.at[i, 0], a2r.at[i, 0], Ap),
            rcopy(part.at[i, 10:12], rA2.at[i, 2:4], a2s.at[i, 1], a2r.at[i, 1], Am),
        )

    def mk_b(i):
        return tuple(
            rcopy(sB.at[i, j], rB.at[i, j], bs.at[i, j], br.at[i, j], dev)
            for j, dev in enumerate((Bp, Bm, B2))
        )

    def mk_c(i):
        return tuple(
            rcopy(G.at[i, 0], G.at[i, j], cs_.at[i, n], cr.at[i, n], dev)
            for n, (j, dev) in enumerate(((3, Bp), (1, Bm), (2, B2)))
        )

    def mk_d1(i):
        return (
            rcopy(G.at[i, 0:4], G.at[i, 12:16], d1s.at[i, 0], d1r.at[i, 0], Ap),
            rcopy(G.at[i, 0:4], G.at[i, 4:8], d1s.at[i, 1], d1r.at[i, 1], Am),
        )

    def mk_d2(i):
        return (
            rcopy(G.at[i, 12:14], G.at[i, 8:10], d2s.at[i, 0], d2r.at[i, 0], Ap),
            rcopy(G.at[i, 6:8], G.at[i, 10:12], d2s.at[i, 1], d2r.at[i, 1], Am),
        )

    def start(pair):
        for c in pair:
            c.start()

    def arrived(pair):
        for c in pair:
            c.wait_recv()

    def a1(i):
        start(mk_a1(i))

    def stage_a2(i):
        arrived(mk_a1(i))
        for j in range(2):
            part[i, 8 + j] = (part[i, 8 + j].astype(F32) + rA1[i, j].astype(F32)).astype(BF)
            part[i, 10 + j] = (part[i, 10 + j].astype(F32) + rA1[i, 4 + j].astype(F32)).astype(BF)
        start(mk_a2(i))

    def stage_b(i):
        arrived(mk_a2(i))
        for b in range(4):
            direct = rA1[i, 6 + b] if b < 2 else rA1[i, b]
            total = part[i, 12 + b].astype(F32) + direct.astype(F32) + rA2[i, b].astype(F32)
            if b == 0:
                sf[i] = total
            else:
                sB[i, (None, 0, 2, 1)[b]] = total.astype(BF)
        if not met:
            met.append(i)
            pl.semaphore_wait(beyond, 2)
        start(mk_b(i))

    def stage_c(i):
        arrived(mk_b(i))
        total = sf[i] + rB[i, 0].astype(F32) + rB[i, 1].astype(F32) + rB[i, 2].astype(F32)
        lc_tok[i].wait()
        scale = lsg[pl.ds(x, 1), :]
        G[i, 0] = (tok[i].astype(F32) + scale * total).astype(BF)
        start(mk_c(i))

    def stage_d1(i):
        arrived(mk_c(i))
        start(mk_d1(i))

    def stage_d2(i):
        arrived(mk_d1(i))
        start(mk_d2(i))

    def send_p(n, dev):
        rcopy(sbuf.at[n], R.at[n], ps.at[n], pr.at[n], dev).start()

    def stage_e(i):
        arrived(mk_d2(i))
        cols = []
        for xg in range(4):
            tiles = []
            for yg in range(4):
                a, b = rel(xg, yg)
                tiles.append(G[i, a * 4 + b])
            cols.append(jnp.concatenate(tiles, axis=0))
        vision = jnp.concatenate(cols, axis=1)
        sorted_rows = jnp.dot(perm[...], vision, preferred_element_type=F32).astype(BF)

        if not waited:
            waited.append(i)
            lc_wm.wait()

        acc = jnp.dot(sorted_rows[:MR], wm[0], preferred_element_type=F32)
        for j in range(1, 4):
            acc = acc + jnp.dot(
                sorted_rows[j * MR : (j + 1) * MR], wm[j], preferred_element_type=F32
            )
        hm = MR // 2

        if i == 0:
            sbuf[0] = acc.astype(BF)
            send_p(0, Z2o)

        if i == 1:
            sbuf[1] = acc.astype(BF)
            send_p(1, Z2)

        for first, n, devs in ((2, 2, (Zpo, Zmo)), (3, 4, (Zp, Zm))):

            if i == first:
                pf[n - 2, :hm] = acc[:hm]
                pf[n - 1, hm:] = acc[hm:]

            if i == first + 2:
                pf[n - 2, hm:] = acc[:hm]
                pf[n - 1, :hm] = acc[hm:]
                sbuf[n] = pf[n - 2].astype(BF)
                sbuf[n + 1] = pf[n - 1].astype(BF)
                send_p(n, devs[0])
                send_p(n + 1, devs[1])

        if i == 6:
            sbuf[6] = acc.astype(BF)
            send_p(6, partner)

        if i == 7:
            pf[4] = acc

    stages = (stage_m, stage_a2, stage_b, stage_c, stage_d1, stage_d2, stage_e)
    waited, met = [], []
    a1(0)
    def tables():
        ri = lax.broadcasted_iota(jnp.int32, (ROWS, ROWS), 0)
        ci = lax.broadcasted_iota(jnp.int32, (ROWS, ROWS), 1)
        perm[...] = jnp.where((ri % MR) * 4 + ri // MR == ci, 1.0, 0.0).astype(BF)
        lc_ls.wait()
        scale_all = ls[...].astype(F32).reshape(1, 4 * TC)
        for g in range(4):
            lsg[g : g + 1, :] = scale_all[:, g * TC : (g + 1) * TC]

        lc_pos.wait()
        prompt_n = choose.shape[0]
        ids = lax.broadcasted_iota(jnp.int32, choose.shape, 0) + col * prompt_n
        hit = jnp.where(pos[...].reshape(1, choose.shape[1]) == ids, 1.0, 0.0)
        choose[...] = hit.astype(BF)
        keep[...] = jnp.broadcast_to(jnp.max(hit, axis=1, keepdims=True), keep.shape)

    for i, n in ORDER[1:]:
        if (i, n) == (2, 0):
            tables()
        if (i, n) == ORDER[-1]:
            early = jnp.zeros(pf.shape[1:], F32)
            for j in range(6):
                rcopy(sbuf.at[j], R.at[j], ps.at[j], pr.at[j], partner).wait_recv()
                early = early + R[j].astype(F32)
            pf[5] = early
        stages[n](i)

    rcopy(sbuf.at[6], R.at[6], ps.at[6], pr.at[6], partner).wait_recv()
    own = zo * 2 + o
    PB[own] = (pf[4] + pf[5] + R[6].astype(F32)).astype(BF)

    def send_f(src, rows, n, dev):
        c = rcopy(PB.at[src, rows], PB.at[src, rows], fs.at[n], fr.at[n], dev)
        return c

    every = pl.ds(0, MR)
    sent = [send_f(own, every, n, dev) for n, dev in enumerate((Z2, Zp, Zm, partner))]
    for c in sent:
        c.start()
    for n, dev, block in ((0, Z2, z), (1, Zp, zp), (2, Zm, zm)):
        send_f(block * 2 + o, every, n, dev).wait_recv()
        onward = send_f(block * 2 + o, every, 4 + n, partner)
        onward.start()
        sent.append(onward)
    for n, block in ((3, zo), (4, z), (5, zp), (6, zm)):
        send_f(block * 2 + k, every, n, partner).wait_recv()

    lc_txt.wait()
    projected = PB[...].reshape(choose.shape[1], PB.shape[2])
    image = jnp.dot(choose[...], projected, preferred_element_type=F32)
    mask = keep[...]
    for g in range(PB.shape[2] // TC):
        cs = slice(g * TC, (g + 1) * TC)
        out[:, cs] = jnp.where(mask > 0.5, image[:, cs].astype(BF), txt[:, cs])

    for c in sent:
        c.wait_send()
    for n in range(7):
        rcopy(sbuf.at[n], R.at[n], ps.at[n], pr.at[n], partner).wait_send()
    for n in range(14):
        rcopy(H.at[0, hpart(0)], H.at[0, hpart(0)], hs.at[n], hr.at[0, 0], partner).wait_send()

    def drain(i, carry):
        for mk in (mk_a1, mk_a2, mk_b, mk_c, mk_d1, mk_d2):
            for c in mk(i):
                c.wait_send()
        return carry

    lax.fori_loop(0, CH, drain, 0)


def per_device(hidden, down_weight, tokens, layer_scale, merge_weight, text_embeds, positions):
    prompt_n, width = text_embeds.shape
    merged = positions.shape[0]
    dma = pltpu.SemaphoreType.DMA
    vm = pltpu.VMEM
    pair = dma((CH, 2))
    return pl.pallas_call(
        kernel,
        out_shape=jax.ShapeDtypeStruct((prompt_n, width), BF),
        in_specs=[pl.BlockSpec(memory_space=pl.ANY)] * 7,
        out_specs=pl.BlockSpec(memory_space=pltpu.VMEM),
        scratch_shapes=[
            vm((CH, ROWS, hidden.shape[1]), BF),
            vm(down_weight.shape, BF),
            vm(merge_weight.shape, BF),
            vm((CH, TR, TC), BF),
            vm(layer_scale.shape, BF),
            vm((8, TC), F32),
            vm((prompt_n, width), BF),
            vm((merged,), jnp.int32),
            vm((ROWS, ROWS), BF),
            vm((prompt_n, merged), BF),
            vm((prompt_n, TC), F32),
            vm((CH, 16, TR, TC), BF),
            vm((CH, 8, TR, TC), BF),
            vm((CH, 4, TR, TC), BF),
            vm((CH, TR, TC), F32),
            vm((CH, 3, TR, TC), BF),
            vm((CH, 3, TR, TC), BF),
            vm((CH, 16, TR, TC), BF),
            vm((6, MR, width), F32),
            vm((7, MR, width), BF),
            vm((7, MR, width), BF),
            vm((8, MR, width), BF),
            dma((13,)),
            dma((14,)),
            pair,
        ]
        + [pair] * 4
        + [dma((CH, 3))] * 4
        + [pair] * 4
        + [dma((7,))] * 4
        + [pltpu.SemaphoreType.REGULAR],
        compiler_params=pltpu.CompilerParams(
            collective_id=0, has_side_effects=True, vmem_limit_bytes=60 * 1024 * 1024
        ),
    )(hidden, down_weight, tokens, layer_scale, merge_weight, text_embeds, positions)


def solution(mesh):
    in_specs = (
        P("col", "row"),
        P("row", "col"),
        P(None, "col"),
        P("col"),
        P(None, "col", "row"),
        P("col", "row"),
        P(),
    )
    return jax.shard_map(
        per_device, mesh=mesh, in_specs=in_specs, out_specs=P("col", "row"), check_vma=False
    )
```

```python
import jax
import jax.numpy as jnp
from jax import lax
from jax.experimental import pallas as pl
from jax.experimental.pallas import tpu as pltpu
from jax.sharding import PartitionSpec as P

MESH = pl.DeviceIdType.MESH
BF = jnp.bfloat16
F32 = jnp.float32
CH = 8
ROWS = 448
HALF = 224
TR, TC = 112, 128
MR = 112

CUT = 64
STRAIGHT = 4
ORDER = (
    (0, 0), (1, 0), (0, 1), (1, 1), (2, 0), (0, 2), (3, 0), (1, 2), (4, 0),
    (2, 1), (0, 3), (5, 0), (3, 1), (1, 3), (0, 4), (6, 0), (4, 1), (2, 2),
    (7, 0), (1, 4), (5, 1), (3, 2), (0, 5), (6, 1), (1, 5), (2, 3), (4, 2),
    (7, 1), (3, 3), (5, 2), (2, 4), (0, 6), (3, 4), (6, 2), (4, 3), (2, 5),
    (1, 6), (5, 3), (7, 2), (3, 5), (0, 7), (6, 3), (2, 6), (4, 5), (5, 5),
    (1, 7), (7, 3), (3, 6), (2, 7), (6, 5), (4, 6), (5, 6), (7, 5), (3, 7),
    (6, 6), (4, 7), (5, 7), (7, 6), (6, 7), (7, 7),
)


def kernel(
    hid, dw, tok_hbm, ls_hbm, mw, txt_hbm, pos_hbm, out,
    H, wd, wm, tok, ls, lsg, txt, pos, perm, choose, keep,
    part, rA1, rA2, sf, sB, rB, G, pf, sbuf, R, PB,
    lsem, hs, hr, a1s, a1r, a2s, a2r, bs, br,
    c1s, c1r, c2s, c2r, d1s, d1r, d2s, d2r, ps, pr, fs, fr, beyond,
):
    row = lax.axis_index("row")
    col = lax.axis_index("col")
    x, y = row // 4, row % 4
    z, k = col // 2, col % 2
    o = 1 - k
    p, q = x + k * (y - x), y + k * (x - y)
    sA, sB_ = 4 - 3 * k, 1 + 3 * k
    zp, zm, zo = (z + 1) % 4, (z + 3) % 4, (z + 2) % 4

    def at_row(r):
        return {"row": r, "col": col}

    def at_col(zz, kk):
        return {"row": row, "col": zz * 2 + kk}

    Ap = at_row(((p + 1) % 4) * sA + q * sB_)
    Am = at_row(((p + 3) % 4) * sA + q * sB_)
    Bp = at_row(p * sA + ((q + 1) % 4) * sB_)
    Bm = at_row(p * sA + ((q + 3) % 4) * sB_)
    B2 = at_row(p * sA + ((q + 2) % 4) * sB_)
    partner = at_col(z, o)
    Zp, Zm = at_col(zp, k), at_col(zm, k)
    Zpo, Zmo = at_col(zp, o), at_col(zm, o)
    Z2, Z2o = at_col(zo, k), at_col(zo, o)

    def rcopy(src, dst, ss, rs, dev):
        return pltpu.make_async_remote_copy(
            src_ref=src, dst_ref=dst, send_sem=ss, recv_sem=rs, device_id=dev, device_id_type=MESH
        )

    def block_row(i):
        yh, yl = y // 2, y % 2
        zs = (z + 3 + 2 * yh) % 4
        if i == 0:
            r = (z * 2 + k) * ROWS + y * TR
        elif i == 1:
            r = (z * 2 + o) * ROWS + y * TR
        elif i < 6:
            kk = k if i % 2 == 0 else o
            r = (zs * 2 + kk) * ROWS + ((yh + i // 4) % 2) * HALF + yl * TR
        else:
            r = (zo * 2 + (k if i == 6 else o)) * ROWS + y * TR
        return pl.multiple_of(r, 16)

    lc_h = [
        pltpu.make_async_copy(hid.at[pl.ds(h * HALF, HALF)], H.at[0, pl.ds(h * HALF, HALF)], hr.at[0, h])
        for h in range(2)
    ]
    lc_wd = pltpu.make_async_copy(dw, wd, lsem.at[0])
    lc_wm = pltpu.make_async_copy(mw, wm, lsem.at[1])
    lc_ls = pltpu.make_async_copy(ls_hbm, ls, lsem.at[2])
    lc_txt = pltpu.make_async_copy(txt_hbm, txt, lsem.at[3])
    lc_pos = pltpu.make_async_copy(pos_hbm, pos, lsem.at[4])
    lane0 = pl.multiple_of(x * TC, TC)
    lc_tok = [
        pltpu.make_async_copy(tok_hbm.at[pl.ds(block_row(i), TR), pl.ds(lane0, TC)], tok.at[i], lsem.at[5 + i])
        for i in range(CH)
    ]
    for c in lc_h:
        c.start()
    lc_wd.start()
    lc_pos.start()
    lc_ls.start()
    for c in lc_tok:
        c.start()
    lc_wm.start()
    lc_txt.start()

    barrier = pltpu.get_barrier_semaphore()
    for dev in (partner, Ap, Am, Bp, Bm, Zp, Zm):
        pl.semaphore_signal(barrier, inc=1, device_id=dev, device_id_type=MESH)

    def hpart(h):
        return pl.ds(h * HALF, HALF)

    def send_h(src, i, h, n, dev):
        rcopy(src, H.at[i, hpart(h)], hs.at[n], hr.at[i, h], dev).start()

    def slot(a, b):
        hi = b // 2
        g = jnp.where(
            a == 0, 12, jnp.where(a == 1, 8 - 8 * hi, jnp.where(a == 2, 2 * hi, 6 + 2 * hi))
        )
        return g + b

    def rel(xg, yg):
        a = xg + k * (yg - xg)
        b = yg + k * (xg - yg)
        return (a + 4 - p) % 4, (b + 4 - q) % 4

    def multiply(i):
        for h in range(2):
            rcopy(H.at[i, hpart(h)], H.at[i, hpart(h)], hs.at[0], hr.at[i, h], partner).wait_recv()
            if i in (2, 4, 6):
                send_h(H.at[i, hpart(h)], i + 1, h, 5 + i // 2 * 2 - 1 + h, partner)
            if i == 2:
                send_h(H.at[2, hpart(h)], 6, h, 12 + h, (Zp, Zm)[h])
        m = jnp.dot(H[i], wd[...], preferred_element_type=F32)
        for yg in range(4):
            for xg in range(4):
                a, b = rel(xg, yg)
                part[i, slot(a, b)] = m[yg * TR : (yg + 1) * TR, xg * TC : (xg + 1) * TC].astype(BF)

    def stage_m(i):
        multiply(i)
        a1(i)

    lc_wd.wait()
    multiply(0)
    pl.semaphore_wait(barrier, 7)
    send_h(hid.at[hpart(0)], 2, 0, 0, Zp)
    send_h(hid.at[hpart(1)], 2, 1, 1, Zm)
    send_h(hid.at[hpart(0)], 1, 0, 2, partner)
    send_h(hid.at[hpart(1)], 1, 1, 3, partner)
    send_h(hid.at[hpart(1)], 4, 0, 4, Zp)
    send_h(hid.at[hpart(0)], 4, 1, 5, Zm)

    for dev in (Bp, Bm):
        pl.semaphore_signal(beyond, inc=1, device_id=dev, device_id_type=MESH)

    def mk_a1(i):
        return (
            rcopy(part.at[i, 0:4], rA1.at[i, 0:4], a1s.at[i, 0], a1r.at[i, 0], Ap),
            rcopy(part.at[i, 4:8], rA1.at[i, 4:8], a1s.at[i, 1], a1r.at[i, 1], Am),
        )

    def mk_a2(i):
        return (
            rcopy(part.at[i, 8:10], rA2.at[i, 0:2], a2s.at[i, 0], a2r.at[i, 0], Ap),
            rcopy(part.at[i, 10:12], rA2.at[i, 2:4], a2s.at[i, 1], a2r.at[i, 1], Am),
        )

    def mk_b(i):
        return tuple(
            rcopy(sB.at[i, j], rB.at[i, j], bs.at[i, j], br.at[i, j], dev)
            for j, dev in enumerate((Bp, Bm, B2))
        )

    lo, hi = pl.ds(0, CUT), pl.ds(CUT, TR - CUT)

    def mk_c1(i):
        pair = (
            rcopy(G.at[i, 0], G.at[i, 3], c1s.at[i, 0], c1r.at[i, 0], Bp),
            rcopy(G.at[i, 0], G.at[i, 1], c1s.at[i, 1], c1r.at[i, 1], Bm),
        )
        if i < STRAIGHT:
            return pair
        return pair + (rcopy(G.at[i, 0], G.at[i, 2], c2s.at[i, 0], c2r.at[i, 0], B2),)

    def mk_c2(i):
        if i >= STRAIGHT:
            return ()
        return (
            rcopy(G.at[i, 3, lo], G.at[i, 2, lo], c2s.at[i, 0], c2r.at[i, 0], Bp),
            rcopy(G.at[i, 1, hi], G.at[i, 2, hi], c2s.at[i, 1], c2r.at[i, 1], Bm),
        )

    def mk_d1(i):
        return (
            rcopy(G.at[i, 0:4], G.at[i, 12:16], d1s.at[i, 0], d1r.at[i, 0], Ap),
            rcopy(G.at[i, 0:4], G.at[i, 4:8], d1s.at[i, 1], d1r.at[i, 1], Am),
        )

    def mk_d2(i):
        return (
            rcopy(G.at[i, 12:14], G.at[i, 8:10], d2s.at[i, 0], d2r.at[i, 0], Ap),
            rcopy(G.at[i, 6:8], G.at[i, 10:12], d2s.at[i, 1], d2r.at[i, 1], Am),
        )

    def start(pair):
        for c in pair:
            c.start()

    def arrived(pair):
        for c in pair:
            c.wait_recv()

    def a1(i):
        start(mk_a1(i))

    def stage_a2(i):
        arrived(mk_a1(i))
        for j in range(2):
            part[i, 8 + j] = (part[i, 8 + j].astype(F32) + rA1[i, j].astype(F32)).astype(BF)
            part[i, 10 + j] = (part[i, 10 + j].astype(F32) + rA1[i, 4 + j].astype(F32)).astype(BF)
        start(mk_a2(i))

    def stage_b(i):
        arrived(mk_a2(i))
        for b in range(4):
            direct = rA1[i, 6 + b] if b < 2 else rA1[i, b]
            total = part[i, 12 + b].astype(F32) + direct.astype(F32) + rA2[i, b].astype(F32)
            if b == 0:
                sf[i] = total
            else:
                sB[i, (None, 0, 2, 1)[b]] = total.astype(BF)
        if not met:
            met.append(i)
            pl.semaphore_wait(beyond, 2)
        start(mk_b(i))

    def stage_c(i):
        arrived(mk_b(i))
        total = sf[i] + rB[i, 0].astype(F32) + rB[i, 1].astype(F32) + rB[i, 2].astype(F32)
        lc_tok[i].wait()
        scale = lsg[pl.ds(x, 1), :]
        G[i, 0] = (tok[i].astype(F32) + scale * total).astype(BF)
        start(mk_c1(i))

    def stage_c2(i):
        arrived(mk_c1(i))
        start(mk_c2(i))

    def stage_d1(i):
        arrived(mk_c2(i) or mk_c1(i))
        start(mk_d1(i))

    def stage_d2(i):
        arrived(mk_d1(i))
        start(mk_d2(i))

    def send_p(n, dev):
        rcopy(sbuf.at[n], R.at[n], ps.at[n], pr.at[n], dev).start()

    def stage_e(i):
        arrived(mk_d2(i))
        cols = []
        for xg in range(4):
            tiles = []
            for yg in range(4):
                a, b = rel(xg, yg)
                tiles.append(G[i, a * 4 + b])
            cols.append(jnp.concatenate(tiles, axis=0))
        vision = jnp.concatenate(cols, axis=1)
        sorted_rows = jnp.dot(perm[...], vision, preferred_element_type=F32).astype(BF)

        if not waited:
            waited.append(i)
            lc_wm.wait()

        acc = jnp.dot(sorted_rows[:MR], wm[0], preferred_element_type=F32)
        for j in range(1, 4):
            acc = acc + jnp.dot(
                sorted_rows[j * MR : (j + 1) * MR], wm[j], preferred_element_type=F32
            )
        hm = MR // 2

        if i == 0:
            sbuf[0] = acc.astype(BF)
            send_p(0, Z2o)

        if i == 1:
            sbuf[1] = acc.astype(BF)
            send_p(1, Z2)

        for first, n, devs in ((2, 2, (Zpo, Zmo)), (3, 4, (Zp, Zm))):

            if i == first:
                pf[n - 2, :hm] = acc[:hm]
                pf[n - 1, hm:] = acc[hm:]

            if i == first + 2:
                pf[n - 2, hm:] = acc[:hm]
                pf[n - 1, :hm] = acc[hm:]
                sbuf[n] = pf[n - 2].astype(BF)
                sbuf[n + 1] = pf[n - 1].astype(BF)
                send_p(n, devs[0])
                send_p(n + 1, devs[1])

        if i == 6:
            sbuf[6] = acc.astype(BF)
            send_p(6, partner)

        if i == 7:
            pf[4] = acc

    stages = (stage_m, stage_a2, stage_b, stage_c, stage_c2, stage_d1, stage_d2, stage_e)
    waited, met = [], []
    a1(0)
    def tables():
        ri = lax.broadcasted_iota(jnp.int32, (ROWS, ROWS), 0)
        ci = lax.broadcasted_iota(jnp.int32, (ROWS, ROWS), 1)
        perm[...] = jnp.where((ri % MR) * 4 + ri // MR == ci, 1.0, 0.0).astype(BF)
        lc_ls.wait()
        scale_all = ls[...].astype(F32).reshape(1, 4 * TC)
        for g in range(4):
            lsg[g : g + 1, :] = scale_all[:, g * TC : (g + 1) * TC]

        lc_pos.wait()
        prompt_n = choose.shape[0]
        ids = lax.broadcasted_iota(jnp.int32, choose.shape, 0) + col * prompt_n
        hit = jnp.where(pos[...].reshape(1, choose.shape[1]) == ids, 1.0, 0.0)
        choose[...] = hit.astype(BF)
        keep[...] = jnp.broadcast_to(jnp.max(hit, axis=1, keepdims=True), keep.shape)

    for i, n in ORDER[1:]:
        if (i, n) == (2, 0):
            tables()
        if (i, n) == ORDER[-1]:
            early = jnp.zeros(pf.shape[1:], F32)
            for j in range(6):
                rcopy(sbuf.at[j], R.at[j], ps.at[j], pr.at[j], partner).wait_recv()
                early = early + R[j].astype(F32)
            pf[5] = early
        stages[n](i)

    rcopy(sbuf.at[6], R.at[6], ps.at[6], pr.at[6], partner).wait_recv()
    own = zo * 2 + o
    PB[own] = (pf[4] + pf[5] + R[6].astype(F32)).astype(BF)

    def send_f(src, rows, n, dev):
        c = rcopy(PB.at[src, rows], PB.at[src, rows], fs.at[n], fr.at[n], dev)
        return c

    every = pl.ds(0, MR)
    sent = [send_f(own, every, n, dev) for n, dev in enumerate((Z2, Zp, Zm, partner))]
    for c in sent:
        c.start()
    for n, dev, block in ((0, Z2, z), (1, Zp, zp), (2, Zm, zm)):
        send_f(block * 2 + o, every, n, dev).wait_recv()
        onward = send_f(block * 2 + o, every, 4 + n, partner)
        onward.start()
        sent.append(onward)
    for n, block in ((3, zo), (4, z), (5, zp), (6, zm)):
        send_f(block * 2 + k, every, n, partner).wait_recv()

    lc_txt.wait()
    projected = PB[...].reshape(choose.shape[1], PB.shape[2])
    image = jnp.dot(choose[...], projected, preferred_element_type=F32)
    mask = keep[...]
    for g in range(PB.shape[2] // TC):
        cs = slice(g * TC, (g + 1) * TC)
        out[:, cs] = jnp.where(mask > 0.5, image[:, cs].astype(BF), txt[:, cs])

    for c in sent:
        c.wait_send()
    for n in range(7):
        rcopy(sbuf.at[n], R.at[n], ps.at[n], pr.at[n], partner).wait_send()
    for n in range(14):
        rcopy(H.at[0, hpart(0)], H.at[0, hpart(0)], hs.at[n], hr.at[0, 0], partner).wait_send()

    for i in range(CH):
        for mk in (mk_a1, mk_a2, mk_b, mk_c1, mk_c2, mk_d1, mk_d2):
            for c in mk(i):
                c.wait_send()


def per_device(hidden, down_weight, tokens, layer_scale, merge_weight, text_embeds, positions):
    prompt_n, width = text_embeds.shape
    merged = positions.shape[0]
    dma = pltpu.SemaphoreType.DMA
    vm = pltpu.VMEM
    pair = dma((CH, 2))
    return pl.pallas_call(
        kernel,
        out_shape=jax.ShapeDtypeStruct((prompt_n, width), BF),
        in_specs=[pl.BlockSpec(memory_space=pl.ANY)] * 7,
        out_specs=pl.BlockSpec(memory_space=pltpu.VMEM),
        scratch_shapes=[
            vm((CH, ROWS, hidden.shape[1]), BF),
            vm(down_weight.shape, BF),
            vm(merge_weight.shape, BF),
            vm((CH, TR, TC), BF),
            vm(layer_scale.shape, BF),
            vm((8, TC), F32),
            vm((prompt_n, width), BF),
            vm((merged,), jnp.int32),
            vm((ROWS, ROWS), BF),
            vm((prompt_n, merged), BF),
            vm((prompt_n, TC), F32),
            vm((CH, 16, TR, TC), BF),
            vm((CH, 8, TR, TC), BF),
            vm((CH, 4, TR, TC), BF),
            vm((CH, TR, TC), F32),
            vm((CH, 3, TR, TC), BF),
            vm((CH, 3, TR, TC), BF),
            vm((CH, 16, TR, TC), BF),
            vm((6, MR, width), F32),
            vm((7, MR, width), BF),
            vm((7, MR, width), BF),
            vm((8, MR, width), BF),
            dma((13,)),
            dma((14,)),
            pair,
        ]
        + [pair] * 4
        + [dma((CH, 3))] * 2
        + [pair] * 8
        + [dma((7,))] * 4
        + [pltpu.SemaphoreType.REGULAR],
        compiler_params=pltpu.CompilerParams(
            collective_id=0, has_side_effects=True, vmem_limit_bytes=60 * 1024 * 1024
        ),
    )(hidden, down_weight, tokens, layer_scale, merge_weight, text_embeds, positions)


def solution(mesh):
    in_specs = (
        P("col", "row"),
        P("row", "col"),
        P(None, "col"),
        P("col"),
        P(None, "col", "row"),
        P("col", "row"),
        P(),
    )
    return jax.shard_map(
        per_device, mesh=mesh, in_specs=in_specs, out_specs=P("col", "row"), check_vma=False
    )
```

```python
import jax
import jax.numpy as jnp
from jax import lax
from jax.experimental import pallas as pl
from jax.experimental.pallas import tpu as pltpu
from jax.sharding import PartitionSpec as P

MESH = pl.DeviceIdType.MESH
BF = jnp.bfloat16
F32 = jnp.float32
CH = 8
ROWS = 448
HALF = 224
TR, TC = 112, 128
MR = 112

CUT = 64
STRAIGHT = 4
ORDER = (
    (0, 0), (1, 0), (0, 1), (1, 1), (2, 0), (0, 2), (3, 0), (1, 2), (4, 0),
    (2, 1), (0, 3), (5, 0), (3, 1), (1, 3), (0, 4), (6, 0), (4, 1), (2, 2),
    (7, 0), (1, 4), (5, 1), (3, 2), (0, 5), (6, 1), (1, 5), (2, 3), (4, 2),
    (7, 1), (3, 3), (5, 2), (2, 4), (0, 6), (3, 4), (6, 2), (4, 3), (2, 5),
    (1, 6), (5, 3), (7, 2), (3, 5), (0, 7), (6, 3), (2, 6), (4, 5), (5, 5),
    (1, 7), (7, 3), (3, 6), (2, 7), (6, 5), (4, 6), (5, 6), (7, 5), (3, 7),
    (6, 6), (4, 7), (5, 7), (7, 6), (6, 7), (7, 7),
)


def kernel(
    hid, dw, tok_hbm, ls_hbm, mw, txt_hbm, pos_hbm, out,
    H, wd, wm, tok, ls, lsg, txt, pos, perm, choose, keep,
    part, rA1, rA2, sf, sB, rB, G, pf, sbuf, R, PB,
    lsem, hs, hr, a1s, a1r, a2s, a2r, bs, br,
    c1s, c1r, c2s, c2r, d1s, d1r, d2s, d2r, ps, pr, fs, fr, beyond,
):
    row = lax.axis_index("row")
    col = lax.axis_index("col")
    x, y = row // 4, row % 4
    z, k = col // 2, col % 2
    o = 1 - k
    p, q = x + k * (y - x), y + k * (x - y)
    sA, sB_ = 4 - 3 * k, 1 + 3 * k
    zp, zm, zo = (z + 1) % 4, (z + 3) % 4, (z + 2) % 4

    def at_row(r):
        return {"row": r, "col": col}

    def at_col(zz, kk):
        return {"row": row, "col": zz * 2 + kk}

    Ap = at_row(((p + 1) % 4) * sA + q * sB_)
    Am = at_row(((p + 3) % 4) * sA + q * sB_)
    Bp = at_row(p * sA + ((q + 1) % 4) * sB_)
    Bm = at_row(p * sA + ((q + 3) % 4) * sB_)
    B2 = at_row(p * sA + ((q + 2) % 4) * sB_)
    partner = at_col(z, o)
    Zp, Zm = at_col(zp, k), at_col(zm, k)
    Zpo, Zmo = at_col(zp, o), at_col(zm, o)
    Z2, Z2o = at_col(zo, k), at_col(zo, o)

    def rcopy(src, dst, ss, rs, dev):
        return pltpu.make_async_remote_copy(
            src_ref=src, dst_ref=dst, send_sem=ss, recv_sem=rs, device_id=dev, device_id_type=MESH
        )

    def block_row(i):
        yh, yl = y // 2, y % 2
        zs = (z + 3 + 2 * yh) % 4
        if i == 0:
            r = (z * 2 + k) * ROWS + y * TR
        elif i == 1:
            r = (z * 2 + o) * ROWS + y * TR
        elif i < 6:
            kk = k if i % 2 == 0 else o
            r = (zs * 2 + kk) * ROWS + ((yh + i // 4) % 2) * HALF + yl * TR
        else:
            r = (zo * 2 + (k if i == 6 else o)) * ROWS + y * TR
        return pl.multiple_of(r, 16)

    lc_h = [
        pltpu.make_async_copy(hid.at[pl.ds(h * HALF, HALF)], H.at[0, pl.ds(h * HALF, HALF)], hr.at[0, h])
        for h in range(2)
    ]
    lc_wd = pltpu.make_async_copy(dw, wd, lsem.at[0])
    lc_wm = pltpu.make_async_copy(mw, wm, lsem.at[1])
    lc_ls = pltpu.make_async_copy(ls_hbm, ls, lsem.at[2])
    lc_txt = pltpu.make_async_copy(txt_hbm, txt, lsem.at[3])
    lc_pos = pltpu.make_async_copy(pos_hbm, pos, lsem.at[4])
    lane0 = pl.multiple_of(x * TC, TC)
    lc_tok = [
        pltpu.make_async_copy(tok_hbm.at[pl.ds(block_row(i), TR), pl.ds(lane0, TC)], tok.at[i], lsem.at[5 + i])
        for i in range(CH)
    ]
    for c in lc_h:
        c.start()
    lc_wd.start()
    lc_pos.start()
    lc_ls.start()
    for c in lc_tok:
        c.start()
    lc_wm.start()
    lc_txt.start()

    barrier = pltpu.get_barrier_semaphore()
    for dev in (partner, Ap, Am, Bp, Bm, Zp, Zm):
        pl.semaphore_signal(barrier, inc=1, device_id=dev, device_id_type=MESH)

    def hpart(h):
        return pl.ds(h * HALF, HALF)

    def send_h(src, i, h, n, dev):
        rcopy(src, H.at[i, hpart(h)], hs.at[n], hr.at[i, h], dev).start()

    def slot(a, b):
        hi = b // 2
        g = jnp.where(
            a == 0, 12, jnp.where(a == 1, 8 - 8 * hi, jnp.where(a == 2, 2 * hi, 6 + 2 * hi))
        )
        return g + b

    def rel(xg, yg):
        a = xg + k * (yg - xg)
        b = yg + k * (xg - yg)
        return (a + 4 - p) % 4, (b + 4 - q) % 4

    def multiply(i):
        for h in range(2):
            rcopy(H.at[i, hpart(h)], H.at[i, hpart(h)], hs.at[0], hr.at[i, h], partner).wait_recv()
            if i in (2, 4, 6):
                send_h(H.at[i, hpart(h)], i + 1, h, 5 + i // 2 * 2 - 1 + h, partner)
            if i == 2:
                send_h(H.at[2, hpart(h)], 6, h, 12 + h, (Zp, Zm)[h])
        m = jnp.dot(H[i], wd[...], preferred_element_type=F32)
        for yg in range(4):
            for xg in range(4):
                a, b = rel(xg, yg)
                part[i, slot(a, b)] = m[yg * TR : (yg + 1) * TR, xg * TC : (xg + 1) * TC].astype(BF)

    def stage_m(i):
        multiply(i)
        a1(i)

    lc_wd.wait()
    multiply(0)
    pl.semaphore_wait(barrier, 7)
    send_h(hid.at[hpart(0)], 2, 0, 0, Zp)
    send_h(hid.at[hpart(1)], 2, 1, 1, Zm)
    send_h(hid.at[hpart(0)], 1, 0, 2, partner)
    send_h(hid.at[hpart(1)], 1, 1, 3, partner)
    send_h(hid.at[hpart(1)], 4, 0, 4, Zp)
    send_h(hid.at[hpart(0)], 4, 1, 5, Zm)

    for dev in (Bp, Bm):
        pl.semaphore_signal(beyond, inc=1, device_id=dev, device_id_type=MESH)

    def mk_a1(i):
        return (
            rcopy(part.at[i, 0:4], rA1.at[i, 0:4], a1s.at[i, 0], a1r.at[i, 0], Ap),
            rcopy(part.at[i, 4:8], rA1.at[i, 4:8], a1s.at[i, 1], a1r.at[i, 1], Am),
        )

    def mk_a2(i):
        return (
            rcopy(part.at[i, 8:10], rA2.at[i, 0:2], a2s.at[i, 0], a2r.at[i, 0], Ap),
            rcopy(part.at[i, 10:12], rA2.at[i, 2:4], a2s.at[i, 1], a2r.at[i, 1], Am),
        )

    def mk_b(i):
        return tuple(
            rcopy(sB.at[i, j], rB.at[i, j], bs.at[i, j], br.at[i, j], dev)
            for j, dev in ((2, B2), (0, Bp), (1, Bm))
        )

    lo, hi = pl.ds(0, CUT), pl.ds(CUT, TR - CUT)

    def mk_c1(i):
        pair = (
            rcopy(G.at[i, 0], G.at[i, 3], c1s.at[i, 0], c1r.at[i, 0], Bp),
            rcopy(G.at[i, 0], G.at[i, 1], c1s.at[i, 1], c1r.at[i, 1], Bm),
        )
        if i < STRAIGHT:
            return pair
        return (rcopy(G.at[i, 0], G.at[i, 2], c2s.at[i, 0], c2r.at[i, 0], B2),) + pair

    def mk_c2(i):
        if i >= STRAIGHT:
            return ()
        return (
            rcopy(G.at[i, 3, lo], G.at[i, 2, lo], c2s.at[i, 0], c2r.at[i, 0], Bp),
            rcopy(G.at[i, 1, hi], G.at[i, 2, hi], c2s.at[i, 1], c2r.at[i, 1], Bm),
        )

    def mk_d1(i):
        return (
            rcopy(G.at[i, 0:4], G.at[i, 12:16], d1s.at[i, 0], d1r.at[i, 0], Ap),
            rcopy(G.at[i, 0:4], G.at[i, 4:8], d1s.at[i, 1], d1r.at[i, 1], Am),
        )

    def mk_d2(i):
        return (
            rcopy(G.at[i, 12:14], G.at[i, 8:10], d2s.at[i, 0], d2r.at[i, 0], Ap),
            rcopy(G.at[i, 6:8], G.at[i, 10:12], d2s.at[i, 1], d2r.at[i, 1], Am),
        )

    def start(pair):
        for c in pair:
            c.start()

    def arrived(pair):
        for c in pair:
            c.wait_recv()

    def a1(i):
        start(mk_a1(i))

    def stage_a2(i):
        arrived(mk_a1(i))
        for j in range(2):
            part[i, 8 + j] = (part[i, 8 + j].astype(F32) + rA1[i, j].astype(F32)).astype(BF)
            part[i, 10 + j] = (part[i, 10 + j].astype(F32) + rA1[i, 4 + j].astype(F32)).astype(BF)
        start(mk_a2(i))

    def stage_b(i):
        arrived(mk_a2(i))
        for b in range(4):
            direct = rA1[i, 6 + b] if b < 2 else rA1[i, b]
            total = part[i, 12 + b].astype(F32) + direct.astype(F32) + rA2[i, b].astype(F32)
            if b == 0:
                sf[i] = total
            else:
                sB[i, (None, 0, 2, 1)[b]] = total.astype(BF)
        if not met:
            met.append(i)
            pl.semaphore_wait(beyond, 2)
        start(mk_b(i))

    def stage_c(i):
        arrived(mk_b(i))
        total = sf[i] + rB[i, 0].astype(F32) + rB[i, 1].astype(F32) + rB[i, 2].astype(F32)
        lc_tok[i].wait()
        scale = lsg[pl.ds(x, 1), :]
        G[i, 0] = (tok[i].astype(F32) + scale * total).astype(BF)
        start(mk_c1(i))

    def stage_c2(i):
        arrived(mk_c1(i))
        start(mk_c2(i))

    def stage_d1(i):
        arrived(mk_c2(i) or mk_c1(i))
        start(mk_d1(i))

    def stage_d2(i):
        arrived(mk_d1(i))
        start(mk_d2(i))

    def send_p(n, dev):
        rcopy(sbuf.at[n], R.at[n], ps.at[n], pr.at[n], dev).start()

    def stage_e(i):
        arrived(mk_d2(i))
        cols = []
        for xg in range(4):
            tiles = []
            for yg in range(4):
                a, b = rel(xg, yg)
                tiles.append(G[i, a * 4 + b])
            cols.append(jnp.concatenate(tiles, axis=0))
        vision = jnp.concatenate(cols, axis=1)
        sorted_rows = jnp.dot(perm[...], vision, preferred_element_type=F32).astype(BF)

        if not waited:
            waited.append(i)
            lc_wm.wait()

        acc = jnp.dot(sorted_rows[:MR], wm[0], preferred_element_type=F32)
        for j in range(1, 4):
            acc = acc + jnp.dot(
                sorted_rows[j * MR : (j + 1) * MR], wm[j], preferred_element_type=F32
            )
        hm = MR // 2

        if i == 0:
            sbuf[0] = acc.astype(BF)
            send_p(0, Z2o)

        if i == 1:
            sbuf[1] = acc.astype(BF)
            send_p(1, Z2)

        for first, n, devs in ((2, 2, (Zpo, Zmo)), (3, 4, (Zp, Zm))):

            if i == first:
                pf[n - 2, :hm] = acc[:hm]
                pf[n - 1, hm:] = acc[hm:]

            if i == first + 2:
                pf[n - 2, hm:] = acc[:hm]
                pf[n - 1, :hm] = acc[hm:]
                sbuf[n] = pf[n - 2].astype(BF)
                sbuf[n + 1] = pf[n - 1].astype(BF)
                send_p(n, devs[0])
                send_p(n + 1, devs[1])

        if i == 6:
            sbuf[6] = acc.astype(BF)
            send_p(6, partner)

        if i == 7:
            pf[4] = acc

    stages = (stage_m, stage_a2, stage_b, stage_c, stage_c2, stage_d1, stage_d2, stage_e)
    waited, met = [], []
    a1(0)
    def tables():
        ri = lax.broadcasted_iota(jnp.int32, (ROWS, ROWS), 0)
        ci = lax.broadcasted_iota(jnp.int32, (ROWS, ROWS), 1)
        perm[...] = jnp.where((ri % MR) * 4 + ri // MR == ci, 1.0, 0.0).astype(BF)
        lc_ls.wait()
        scale_all = ls[...].astype(F32).reshape(1, 4 * TC)
        for g in range(4):
            lsg[g : g + 1, :] = scale_all[:, g * TC : (g + 1) * TC]

        lc_pos.wait()
        prompt_n = choose.shape[0]
        ids = lax.broadcasted_iota(jnp.int32, choose.shape, 0) + col * prompt_n
        hit = jnp.where(pos[...].reshape(1, choose.shape[1]) == ids, 1.0, 0.0)
        choose[...] = hit.astype(BF)
        keep[...] = jnp.broadcast_to(jnp.max(hit, axis=1, keepdims=True), keep.shape)

    for i, n in ORDER[1:]:
        if (i, n) == (2, 0):
            tables()
        if (i, n) == ORDER[-1]:
            early = jnp.zeros(pf.shape[1:], F32)
            for j in range(6):
                rcopy(sbuf.at[j], R.at[j], ps.at[j], pr.at[j], partner).wait_recv()
                early = early + R[j].astype(F32)
            pf[5] = early
        stages[n](i)

    rcopy(sbuf.at[6], R.at[6], ps.at[6], pr.at[6], partner).wait_recv()
    own = zo * 2 + o
    PB[own] = (pf[4] + pf[5] + R[6].astype(F32)).astype(BF)

    def send_f(src, rows, n, dev):
        c = rcopy(PB.at[src, rows], PB.at[src, rows], fs.at[n], fr.at[n], dev)
        return c

    every = pl.ds(0, MR)
    sent = [send_f(own, every, n, dev) for n, dev in enumerate((Z2, Zp, Zm, partner))]
    for c in sent:
        c.start()
    for n, dev, block in ((0, Z2, z), (1, Zp, zp), (2, Zm, zm)):
        send_f(block * 2 + o, every, n, dev).wait_recv()
        onward = send_f(block * 2 + o, every, 4 + n, partner)
        onward.start()
        sent.append(onward)
    for n, block in ((3, zo), (4, z), (5, zp), (6, zm)):
        send_f(block * 2 + k, every, n, partner).wait_recv()

    lc_txt.wait()
    projected = PB[...].reshape(choose.shape[1], PB.shape[2])
    image = jnp.dot(choose[...], projected, preferred_element_type=F32)
    mask = keep[...]
    for g in range(PB.shape[2] // TC):
        cs = slice(g * TC, (g + 1) * TC)
        out[:, cs] = jnp.where(mask > 0.5, image[:, cs].astype(BF), txt[:, cs])

    for c in sent:
        c.wait_send()
    for n in range(7):
        rcopy(sbuf.at[n], R.at[n], ps.at[n], pr.at[n], partner).wait_send()
    for n in range(14):
        rcopy(H.at[0, hpart(0)], H.at[0, hpart(0)], hs.at[n], hr.at[0, 0], partner).wait_send()

    for i in range(CH):
        for mk in (mk_a1, mk_a2, mk_b, mk_c1, mk_c2, mk_d1, mk_d2):
            for c in mk(i):
                c.wait_send()


def per_device(hidden, down_weight, tokens, layer_scale, merge_weight, text_embeds, positions):
    prompt_n, width = text_embeds.shape
    merged = positions.shape[0]
    dma = pltpu.SemaphoreType.DMA
    vm = pltpu.VMEM
    pair = dma((CH, 2))
    return pl.pallas_call(
        kernel,
        out_shape=jax.ShapeDtypeStruct((prompt_n, width), BF),
        in_specs=[pl.BlockSpec(memory_space=pl.ANY)] * 7,
        out_specs=pl.BlockSpec(memory_space=pltpu.VMEM),
        scratch_shapes=[
            vm((CH, ROWS, hidden.shape[1]), BF),
            vm(down_weight.shape, BF),
            vm(merge_weight.shape, BF),
            vm((CH, TR, TC), BF),
            vm(layer_scale.shape, BF),
            vm((8, TC), F32),
            vm((prompt_n, width), BF),
            vm((merged,), jnp.int32),
            vm((ROWS, ROWS), BF),
            vm((prompt_n, merged), BF),
            vm((prompt_n, TC), F32),
            vm((CH, 16, TR, TC), BF),
            vm((CH, 8, TR, TC), BF),
            vm((CH, 4, TR, TC), BF),
            vm((CH, TR, TC), F32),
            vm((CH, 3, TR, TC), BF),
            vm((CH, 3, TR, TC), BF),
            vm((CH, 16, TR, TC), BF),
            vm((6, MR, width), F32),
            vm((7, MR, width), BF),
            vm((7, MR, width), BF),
            vm((8, MR, width), BF),
            dma((13,)),
            dma((14,)),
            pair,
        ]
        + [pair] * 4
        + [dma((CH, 3))] * 2
        + [pair] * 8
        + [dma((7,))] * 4
        + [pltpu.SemaphoreType.REGULAR],
        compiler_params=pltpu.CompilerParams(
            collective_id=0, has_side_effects=True, vmem_limit_bytes=60 * 1024 * 1024
        ),
    )(hidden, down_weight, tokens, layer_scale, merge_weight, text_embeds, positions)


def solution(mesh):
    in_specs = (
        P("col", "row"),
        P("row", "col"),
        P(None, "col"),
        P("col"),
        P(None, "col", "row"),
        P("col", "row"),
        P(),
    )
    return jax.shard_map(
        per_device, mesh=mesh, in_specs=in_specs, out_specs=P("col", "row"), check_vma=False
    )
```
